32 devices in a mesh: orb: 8 (over z, x), grid: 4 (over y, core).
Axes of the slice: x: 2, y: 2, z: 4, core: 2. Of those that a mesh axis runs over, the one named last changes fastest.
Arguments:
- potentials: float32 [8, 2, 4, 64, 1024], P('orb', None, None, 'grid'), may hold values from -6 to 6
- orbitals: float32 [32, 64, 1024], P('orb', 'grid'), may hold values from -6 to 6
- local_pot: float32 [64, 1024], P('grid'), may hold values from 0 to 1
- shifts: float32 [32], P('orb'), may hold values from 0.75 to 2
- occupation: int32 [32], P('orb'), may hold values from 1 to 2
- owner: int32 [2], replicated, may hold values from 0 to 7
Outputs:
- response: float32 [8, 2, 4, 64, 1024], P('orb', None, None, 'grid')
The draws below stay inside these ranges and needn't reach their ends.
All inputs are finite; a program needn't handle non-finite values.
Results may differ from the reference program's by a relative error of at most 0.00002.
Values sent between devices are 32-bit elements; how exact they have to be, the bound alone decides.
A program may use at most 64 MiB of HBM per device.

```python
import math
import jax
import jax.numpy as jnp
from jax import lax

NZ = 32
TRIAL = 4
BLOCKS = 2
ITERS = 4
PLANE = 1024
NX = 64
ORBITALS = 32
SLOTS = 8


def place_ends(array, rng, least, top_value):
    index_at = [jax.random.randint(jax.random.fold_in(rng, axis), (), 0, length) for axis, length in enumerate(array.shape)]
    main_axis = array.shape.index(max(array.shape))
    next_to = index_at[:main_axis] + [(index_at[main_axis] + 1) % array.shape[main_axis]] + index_at[main_axis + 1:]
    return array.at[tuple(index_at)].set(least).at[tuple(next_to)].set(top_value)


def levels(rng, extent, cuts, smallest, largest):
    loudness = 1.0
    for position, parts in cuts:
        steps = jax.random.uniform(jax.random.fold_in(jax.random.fold_in(rng, 6), position), (parts,), jnp.float32, smallest / len(cuts), largest / len(cuts))
        loudness = loudness * jnp.repeat(jnp.exp(steps), extent[position] // parts).reshape((-1,) + (1,) * (len(extent) - 1 - position))
    return loudness


def bell_draw(stream_key, shape, spread, bound, split=(), kind=jnp.bfloat16):
    array = jax.random.normal(stream_key, shape, jnp.float32) * spread
    if len(split) > 0:
        array = levels(stream_key, shape, split, -0.22, 0.18) * array
    return jnp.clip(array, min=-bound, max=bound).astype(kind)


def setup_inputs(seed: int = 0) -> dict:
    keys = jax.random.split(jax.random.key(seed), 7)
    return {
        "potentials": bell_draw(keys[0], (SLOTS, BLOCKS, TRIAL, NX, PLANE), 1.0, 6.0, ((0, 8), (3, 4)), jnp.float32),
        "orbitals": bell_draw(keys[1], (ORBITALS, NX, PLANE), 1.0, 6.0, ((0, 8), (1, 4)), jnp.float32),
        "local_pot": jnp.clip(1.0 * jax.random.uniform(keys[2], (NX, PLANE), jnp.float32) ** levels(keys[2], (NX, PLANE), ((0, 4),), -0.2, 0.2), 0.0, 1.0),
        "shifts": jnp.clip(jnp.exp(math.log(2.0) - 0.98082925 * jax.random.uniform(keys[3], (ORBITALS,), jnp.float32) ** levels(keys[3], (ORBITALS,), ((0, 8),), -0.2, 0.2)), 0.75, 2.0),
        "occupation": place_ends(jax.random.randint(keys[4], (ORBITALS,), 1, 3), jax.random.fold_in(keys[4], 1), 1, 2).astype(jnp.int32),
        "owner": jax.random.randint(keys[5], (BLOCKS,), 0, SLOTS).astype(jnp.int32),
    }


NEAR_COEF = 4.0 / 3.0
FAR_COEF = -1.0 / 12.0
CENTER_COEF = -2.5
KINETIC_DIAG = 3.75


def laplacian(padded, solution):
    cell_rows = solution.shape[-2]
    plane_cells = solution.shape[-1]
    along_rows = NEAR_COEF * (padded[..., 1:cell_rows + 1, :] + padded[..., 3:cell_rows + 3, :]) + FAR_COEF * (padded[..., 0:cell_rows, :] + padded[..., 4:cell_rows + 4, :])
    widths = [(0, 0)] * (solution.ndim - 1)
    padded_cols = jnp.pad(solution, widths + [(2 * NZ, 2 * NZ)])
    along_cols = NEAR_COEF * (padded_cols[..., NZ:NZ + plane_cells] + padded_cols[..., 3 * NZ:3 * NZ + plane_cells]) + FAR_COEF * (padded_cols[..., 0:plane_cells] + padded_cols[..., 4 * NZ:4 * NZ + plane_cells])
    padded_depth = jnp.pad(solution, widths + [(2, 2)])
    z_index = jnp.arange(plane_cells, dtype=jnp.int32) % NZ
    lower_one = (z_index >= 1).astype(solution.dtype)
    upper_one = (z_index <= NZ - 2).astype(solution.dtype)
    lower_two = (z_index >= 2).astype(solution.dtype)
    upper_two = (z_index <= NZ - 3).astype(solution.dtype)
    along_depth = NEAR_COEF * (padded_depth[..., 1:plane_cells + 1] * lower_one + padded_depth[..., 3:plane_cells + 3] * upper_one) + FAR_COEF * (padded_depth[..., 0:plane_cells] * lower_two + padded_depth[..., 4:plane_cells + 4] * upper_two)
    return along_rows + along_cols + along_depth + 3.0 * CENTER_COEF * solution


def sweep(padded, solution, source, potential, diagonal):
    applied = -0.5 * laplacian(padded, solution) + potential * solution
    return solution + (source - applied) / diagonal


def reference(potentials, orbitals, local_pot, shifts, occupation, owner):
    slot_ids = jnp.arange(SLOTS, dtype=jnp.int32)
    chosen_slot = (slot_ids[:, None] == owner[None, :]).astype(jnp.float32)
    block_ids = jnp.arange(BLOCKS, dtype=jnp.int32)
    trials = potentials[owner, block_ids].reshape(BLOCKS * TRIAL, NX, PLANE)

    def one_orbital(accumulated, inputs):
        orbital, shift_value, weight = inputs
        source = -(trials * orbital[None])
        potential = local_pot + shift_value
        diagonal = KINETIC_DIAG + potential
        solution = source / diagonal
        for repeat in range(ITERS):
            padded = jnp.pad(solution, ((0, 0), (2, 2), (0, 0)))
            solution = sweep(padded, solution, source, potential, diagonal)
        return accumulated + weight.astype(jnp.float32) * orbital[None] * solution, None

    start_sum = jnp.zeros((BLOCKS * TRIAL, NX, PLANE), jnp.float32)
    accumulated, unused = lax.scan(one_orbital, start_sum, (orbitals, shifts, occupation))
    density = accumulated.reshape(BLOCKS, TRIAL, NX, PLANE)
    return chosen_slot[:, :, None, None, None] * density[None]
```

```python
import functools

import jax
import jax.numpy as jnp
from jax import lax
from jax.experimental import pallas as pl
from jax.experimental.pallas import tpu as pltpu
from jax.sharding import PartitionSpec as P

NZ = 32
ITERS = 4
REACH = 2
HALO = REACH * ITERS
KINETIC_DIAG = 3.75
PAIR = 2
MESH = pl.DeviceIdType.MESH


class Ring:
    def __init__(self, count, grids):
        self.count, self.lines, self.grids = count, count // PAIR, grids
        self.me = lax.axis_index("orb")
        self.row = lax.axis_index("grid")
        self.line, self.side = self.me // PAIR, self.me % PAIR
        self.partner = self.line * PAIR + (1 - self.side)

    def at_line(self, line):
        return {"orb": line * PAIR + self.side, "grid": self.row}

    def across(self):
        return {"orb": self.partner, "grid": self.row}

    def up(self):
        return {"orb": self.me, "grid": self.row - 1}

    def down(self):
        return {"orb": self.me, "grid": self.row + 1}


def enter(ring, with_grid):
    barrier = pltpu.get_barrier_semaphore()
    top = ring.lines - 1

    def greet(target):
        pl.semaphore_signal(barrier, inc=1, device_id=target, device_id_type=MESH)

    greet(ring.across())

    @pl.when(ring.line > 0)
    def _():
        greet(ring.at_line(ring.line - 1))

    @pl.when(ring.line < top)
    def _():
        greet(ring.at_line(ring.line + 1))

    peers = 1 + (ring.line + top) // ring.lines + (2 * top - ring.line) // ring.lines
    if with_grid:

        @pl.when(ring.row > 0)
        def _():
            greet(ring.up())

        @pl.when(ring.row < ring.grids - 1)
        def _():
            greet(ring.down())

        last = ring.grids - 1
        peers = peers + (ring.row + last) // ring.grids + (2 * last - ring.row) // ring.grids
    pl.semaphore_wait(barrier, peers)


def send(src, dst, send_sem, recv_sem, target):
    return pltpu.make_async_remote_copy(
        src_ref=src, dst_ref=dst, send_sem=send_sem, recv_sem=recv_sem,
        device_id=target, device_id_type=MESH,
    )


LAG = 4
SUB = 8
LANES = 128
WIDTH = 256


class Waves:
    def __init__(self, ring, chunks, buffers, sems):
        self.ring, self.chunks, self.sems = ring, chunks, sems
        self.from_left, self.from_right, self.to_right, self.to_left = buffers
        self.has_left, self.has_right = ring.line > 0, ring.line < ring.lines - 1

    def right(self, q, target):
        sems = self.sems
        return send(self.to_right.at[q], self.from_left.at[q], sems.at[0, q], sems.at[1, q], target)

    def left(self, q, target):
        sems = self.sems
        return send(self.to_left.at[q], self.from_right.at[q], sems.at[2, q], sems.at[3, q], target)

    def clear(self):
        @pl.when(jnp.logical_not(self.has_left))
        def _():
            self.from_left[...] = jnp.zeros_like(self.from_left)

        @pl.when(jnp.logical_not(self.has_right))
        def _():
            self.from_right[...] = jnp.zeros_like(self.from_right)

    def begin(self, q, value):
        @pl.when(jnp.logical_not(self.has_left) & self.has_right)
        def _():
            self.to_right[q] = value
            self.right(q, self.ring.at_line(self.ring.line + 1)).start()

        @pl.when(jnp.logical_not(self.has_right) & self.has_left)
        def _():
            self.to_left[q] = value
            self.left(q, self.ring.at_line(self.ring.line - 1)).start()

    def run(self, prepare, onward, finish):
        ring, line, top = self.ring, self.ring.line, self.ring.lines - 1
        beyond = (2 * line) // ring.lines
        late = beyond * line + (1 - beyond) * (top - line)

        def step(s, carry):
            def event(offset, act):
                q = s - offset

                @pl.when((q >= 0) & (q < self.chunks))
                def _():
                    act(q)

            def rightward(q):
                @pl.when(self.has_left)
                def _():
                    self.right(q, ring.across()).wait_recv()

                @pl.when(self.has_left & self.has_right)
                def _():
                    self.to_right[q] = onward(q, self.from_left[q])
                    self.right(q, ring.at_line(line + 1)).start()

            def leftward(q):
                @pl.when(self.has_right)
                def _():
                    self.left(q, ring.across()).wait_recv()

                @pl.when(self.has_left & self.has_right)
                def _():
                    self.to_left[q] = onward(q, self.from_right[q])
                    self.left(q, ring.at_line(line - 1)).start()

            event(0, prepare)
            event(line * LAG, rightward)
            event((top - line) * LAG, leftward)
            event(late * LAG, finish)
            return carry

        lax.fori_loop(0, self.chunks + top * LAG, step, 0)

    def drain(self):
        @pl.when(self.has_right)
        def _():
            for q in range(self.chunks):
                self.right(q, self.ring.across()).wait_send()

        @pl.when(self.has_left)
        def _():
            for q in range(self.chunks):
                self.left(q, self.ring.across()).wait_send()


def chunk_of(ref, q, per, start=0):
    return ref.at[q // per, pl.ds(pl.multiple_of(start + (q % per) * HALO, HALO), HALO)]


def band_matrix(depth, width):
    k = lax.broadcasted_iota(jnp.int32, (depth, width), 0)
    n = lax.broadcasted_iota(jnp.int32, (depth, width), 1) + width // 2
    far_y, far_z = jnp.abs(k // NZ - n // NZ), jnp.abs(k % NZ - n % NZ)
    near = ((far_y == 1) & (far_z == 0)) | ((far_y == 0) & (far_z == 1))
    far = ((far_y == 2) & (far_z == 0)) | ((far_y == 0) & (far_z == 2))
    return jnp.where(near, 16.0, jnp.where(far, -1.0, 0.0)).astype(jnp.bfloat16)


def split(value):
    high = value.astype(jnp.bfloat16)
    return high, (value - high.astype(jnp.float32)).astype(jnp.bfloat16)


class Sweeps:
    def __init__(self, trial, orbs, local, pack, density, scratch):
        self.trial, self.orbs, self.local, self.pack, self.density = trial, orbs, local, pack, density
        (
            self.first, self.scale, self.source, self.weighted, self.now_a, self.now_b,
            self.hi_a, self.hi_b, self.lo_a, self.lo_b, self.product, self.band,
        ) = scratch
        self.orbitals = orbs.shape[0] // PAIR
        self.planes, self.cells = local.shape
        self.group = SUB // self.orbitals

    def start(self):
        self.band[...] = band_matrix(2 * WIDTH, WIDTH)
        self.density[...] = jnp.zeros_like(self.density)

    def prepare(self, k, has_up, has_down):
        planes, cells, orbitals = self.planes, self.cells, self.orbitals
        rows = planes - 2 * HALO
        shift = jnp.broadcast_to(self.pack[k, 0:SUB, 0:1], (SUB, cells))
        weight = jnp.broadcast_to(self.pack[k, SUB : 2 * SUB, 0:1], (SUB, cells))
        which = lax.broadcasted_iota(jnp.int32, (SUB, cells), 0) % orbitals
        for p in range(planes):
            orb = jnp.broadcast_to(self.orbs[k * orbitals, p : p + 1, :], (SUB, cells))
            for n in range(1, orbitals):
                other = jnp.broadcast_to(self.orbs[k * orbitals + n, p : p + 1, :], (SUB, cells))
                orb = jnp.where(which < n, orb, other)
            here = jnp.broadcast_to(self.local[p : p + 1, :], (SUB, cells))
            inverse = 1.0 / (KINETIC_DIAG + (here + shift))
            if p < HALO:
                inverse = jnp.where(has_up, inverse, 0.0)
            if p >= HALO + rows:
                inverse = jnp.where(has_down, inverse, 0.0)
            self.scale[p] = inverse * (1.0 / 24.0)
            self.source[p] = -(orb * inverse)
            if HALO <= p < HALO + rows:
                self.weighted[p - HALO] = weight * orb

    def run(self, tau):
        planes, cells, first, scale = self.planes, self.cells, self.first, self.scale
        batch, group, orbitals = SUB, self.group, self.orbitals
        rows = planes - 2 * HALO
        which = lax.broadcasted_iota(jnp.int32, (batch, cells), 0) // orbitals
        for x in range(0, planes, 2):
            values = []
            for p in (x, x + 1):
                trial = jnp.broadcast_to(self.trial[tau * group, pl.ds(p, 1), :], (batch, cells))
                for j in range(1, group):
                    other = jnp.broadcast_to(self.trial[tau * group + j, pl.ds(p, 1), :], (batch, cells))
                    trial = jnp.where(which < j, trial, other)
                value = trial * self.source[p]
                first[p] = value
                values.append(value)
            high, low = split(jnp.concatenate(values, axis=0))
            self.hi_a[x * batch : (x + 2) * batch] = high
            self.lo_a[x * batch : (x + 2) * batch] = low
        current = first
        buffers = ((self.now_a, self.hi_a, self.lo_a), (self.now_b, self.hi_b, self.lo_b))
        product = self.product
        for repeat in range(ITERS):
            hi_in, lo_in = buffers[repeat % 2][1:]
            target, hi_out, lo_out = buffers[(repeat + 1) % 2]
            margin = REACH * (repeat + 1)
            extent = planes - 2 * margin
            for left in range(0, cells, WIDTH):
                a = max(0, left - WIDTH // 2)
                b = min(cells, left + WIDTH + WIDTH // 2)
                k = a - (left - WIDTH // 2)
                weights = self.band[k : k + b - a, :]
                span = slice(margin * batch, (margin + extent) * batch)
                product[0 : extent * batch] = jnp.dot(
                    hi_in[span, a:b], weights, preferred_element_type=jnp.float32
                ) + jnp.dot(lo_in[span, a:b], weights, preferred_element_type=jnp.float32)
                lanes = slice(left, left + WIDTH)
                for x in range(margin, margin + extent, 2):
                    values = []
                    for p in (x, x + 1):
                        near = current[p - 1, :, lanes] + current[p + 1, :, lanes]
                        far = current[p - 2, :, lanes] + current[p + 2, :, lanes]
                        spot = (p - margin) * batch
                        moved = product[spot : spot + batch] + (16.0 * near - far)
                        value = first[p, :, lanes] + scale[p, :, lanes] * moved
                        if repeat == ITERS - 1:
                            where = pl.ds(pl.multiple_of((tau * rows + p - margin) * batch, batch), batch)
                            term = self.weighted[p - margin, :, lanes] * value
                            for c in range(WIDTH // LANES):
                                block = left // LANES + c
                                self.density[block, where, :] += term[:, c * LANES : (c + 1) * LANES]
                        else:
                            target[p, :, lanes] = value
                            values.append(value)
                    if values:
                        high, low = split(jnp.concatenate(values, axis=0))
                        hi_out[x * batch : (x + 2) * batch, lanes] = high
                        lo_out[x * batch : (x + 2) * batch, lanes] = low
            current = target

    def collect(self, t, c):
        rows = self.planes - 2 * HALO
        tau, j = t // self.group, t % self.group
        base = (tau * rows + c * HALO) * SUB + j * self.orbitals
        pieces = []
        for block in range(self.cells // LANES):
            total = self.density[block, pl.ds(base, HALO, stride=SUB), :]
            for n in range(1, self.orbitals):
                total = total + self.density[block, pl.ds(base + n, HALO, stride=SUB), :]
            pieces.append(total)
        return jnp.concatenate(pieces, axis=1)


def respond_kernel(
    count, grids, kinds, owner_ref, shift_ref, weight_ref, pot_ref, orb_ref, local_ref, out_ref,
    mine, crossed, merged, trial, orbs, local, pack, part, density,
    s_left, s_right, s_rightward, s_leftward, r_left, r_right, r_rightward, r_leftward,
    first, scale, source, weighted, now_a, now_b, hi_a, hi_b, lo_a, lo_b, product, band,
    load_sems, cross_sems, s_sems, r_sems, halo_sems, edge_sems, pair_sems, side_sems,
):
    ring = Ring(count, grids)
    orbitals, rows, cells = orb_ref.shape
    half = pot_ref.shape[1]
    per = rows // HALO
    chunks = half * per
    last = HALO + rows
    has_up, has_down = ring.row > 0, ring.row < grids - 1
    spread = Waves(ring, chunks, (s_left, s_right, s_rightward, s_leftward), s_sems)
    gather = Waves(ring, chunks, (r_left, r_right, r_rightward, r_leftward), r_sems)
    sweeps = Sweeps(
        trial, orbs, local, pack, density,
        (first, scale, source, weighted, now_a, now_b, hi_a, hi_b, lo_a, lo_b, product, band),
    )
    group = sweeps.group
    pairs = half // group

    def orb_rows(k, n, start, size):
        return orbs.at[k * orbitals + n, pl.ds(start, size)]

    loads = [
        pltpu.make_async_copy(pot_ref.at[ring.side], mine, load_sems.at[0]),
        pltpu.make_async_copy(local_ref, local.at[pl.ds(HALO, rows)], load_sems.at[1]),
    ] + [
        pltpu.make_async_copy(orb_ref.at[n], orb_rows(0, n, HALO, rows), load_sems.at[2 + n])
        for n in range(orbitals)
    ]
    for load in loads:
        load.start()
    for s in range(SUB):
        n = s % orbitals
        pack[0, s] = jnp.full((LANES,), shift_ref[n], jnp.float32)
        pack[0, SUB + s] = jnp.full((LANES,), weight_ref[n].astype(jnp.float32), jnp.float32)
    spread.clear()
    gather.clear()

    def clear(start):
        orbs[:, start : start + HALO] = jnp.zeros((PAIR * orbitals, HALO, cells), jnp.float32)
        local[start : start + HALO] = jnp.zeros((HALO, cells), jnp.float32)
        trial[:, start : start + HALO] = jnp.zeros((half, HALO, cells), jnp.float32)

    @pl.when(jnp.logical_not(has_up))
    def _():
        clear(0)

    @pl.when(jnp.logical_not(has_down))
    def _():
        clear(last)

    enter(ring, True)

    def cross(q):
        return send(
            chunk_of(pot_ref.at[1 - ring.side], q, per), crossed.at[q],
            cross_sems.at[0, q], cross_sems.at[1, q], ring.across(),
        )

    for q in range(chunks):
        cross(q).start()
    share = send(pack.at[0], pack.at[1], pair_sems.at[0, orbitals], pair_sems.at[1, orbitals], ring.across())
    share.start()

    def center(n):
        return send(
            orb_ref.at[n], orb_rows(1, n, HALO, rows),
            pair_sems.at[0, n], pair_sems.at[1, n], ring.across(),
        )

    for n in range(orbitals):
        center(n).start()

    def edge_up(k, target):
        if k == 0:
            src, dst = local_ref.at[pl.ds(0, HALO)], local.at[pl.ds(last, HALO)]
        elif k <= orbitals:
            src, dst = orb_ref.at[k - 1, pl.ds(0, HALO)], orb_rows(0, k - 1, last, HALO)
        else:
            n = k - 1 - orbitals
            src, dst = orb_rows(1, n, HALO, HALO), orb_rows(1, n, last, HALO)
        return send(src, dst, edge_sems.at[0, 0, k], edge_sems.at[1, 0, k], target)

    def edge_down(k, target):
        if k == 0:
            src, dst = local_ref.at[pl.ds(rows - HALO, HALO)], local.at[pl.ds(0, HALO)]
        elif k <= orbitals:
            src, dst = orb_ref.at[k - 1, pl.ds(rows - HALO, HALO)], orb_rows(0, k - 1, 0, HALO)
        else:
            n = k - 1 - orbitals
            src, dst = orb_rows(1, n, rows, HALO), orb_rows(1, n, 0, HALO)
        return send(src, dst, edge_sems.at[0, 1, k], edge_sems.at[1, 1, k], target)

    own = range(0, 1 + orbitals)
    theirs = range(1 + orbitals, 1 + 2 * orbitals)

    def start_edges(which):
        @pl.when(has_up)
        def _():
            for k in which:
                edge_up(k, ring.up()).start()

        @pl.when(has_down)
        def _():
            for k in which:
                edge_down(k, ring.down()).start()

    def await_edges(which):
        @pl.when(has_up)
        def _():
            for k in which:
                edge_down(k, ring.across()).wait_recv()

        @pl.when(has_down)
        def _():
            for k in which:
                edge_up(k, ring.across()).wait_recv()

    start_edges(own)
    sweeps.start()
    loads[0].wait()

    def owner_of(q):
        return owner_ref[(ring.side * half + q // per) // kinds]

    def halo_up(t, target):
        return send(
            trial.at[t, pl.ds(HALO, HALO)], trial.at[t, pl.ds(last, HALO)],
            halo_sems.at[0, 0, t], halo_sems.at[1, 0, t], target,
        )

    def halo_down(t, target):
        return send(
            trial.at[t, pl.ds(rows, HALO)], trial.at[t, pl.ds(0, HALO)],
            halo_sems.at[0, 1, t], halo_sems.at[1, 1, t], target,
        )

    def merge(q):
        cross(q).wait_recv()
        value = jnp.where(owner_of(q) == ring.partner, crossed[q], chunk_of(mine, q, per)[...])
        merged[q] = value
        spread.begin(q, jnp.where(owner_of(q) // PAIR == ring.line, value, 0.0))

    def select(q, came):
        return jnp.where(owner_of(q) // PAIR == ring.line, merged[q], came)

    def settle(q):
        place = owner_of(q) // PAIR
        other = jnp.where(place < ring.line, s_left[q], s_right[q])
        chunk_of(trial, q, per, HALO)[...] = jnp.where(place == ring.line, merged[q], other)

        @pl.when(has_up & (q % per == 0))
        def _():
            halo_up(q // per, ring.up()).start()

        @pl.when(has_down & (q % per == per - 1))
        def _():
            halo_down(q // per, ring.down()).start()

    spread.run(merge, select, settle)

    def item(i, carry):
        k, tau = i // pairs, i % pairs

        @pl.when(i == 0)
        def _():
            for load in loads[1:]:
                load.wait()
            await_edges(own)

        @pl.when(i == pairs)
        def _():
            await_edges(theirs)

        @pl.when(tau == 0)
        def _():
            sweeps.prepare(k, has_up, has_down)

        @pl.when(i == 0)
        def _():
            for n in range(orbitals):
                center(n).wait_recv()
            share.wait_recv()
            start_edges(theirs)

        @pl.when(k == 0)
        def _():
            @pl.when(has_up)
            def _():
                for j in range(group):
                    halo_down(tau * group + j, ring.across()).wait_recv()

            @pl.when(has_down)
            def _():
                for j in range(group):
                    halo_up(tau * group + j, ring.across()).wait_recv()

        sweeps.run(tau)

        @pl.when(k == PAIR - 1)
        def _():
            for j in range(group):
                for c in range(per):
                    t = tau * group + j
                    value = sweeps.collect(t, c)
                    part[t, c * HALO : (c + 1) * HALO] = value
                    gather.begin(t * per + c, value)

        return carry

    lax.fori_loop(0, PAIR * pairs, item, 0)

    ours, other = out_ref.at[ring.side], out_ref.at[1 - ring.side]

    def across(view, q):
        piece = chunk_of(view, q, per)
        return send(piece, piece, side_sems.at[0, q], side_sems.at[1, q], ring.across())

    def add(q, came):
        return came + chunk_of(part, q, per)[...]

    def finish(q):
        total = r_left[q] + chunk_of(part, q, per)[...] + r_right[q]
        chunk_of(ours, q, per)[...] = total
        across(ours, q).start()

    gather.run(lambda q: None, add, finish)

    def sent(which):
        @pl.when(has_up)
        def _():
            for k in which:
                edge_up(k, ring.across()).wait_send()

        @pl.when(has_down)
        def _():
            for k in which:
                edge_down(k, ring.across()).wait_send()

    sent(own)
    sent(theirs)

    @pl.when(has_up)
    def _():
        for t in range(half):
            halo_up(t, ring.across()).wait_send()

    @pl.when(has_down)
    def _():
        for t in range(half):
            halo_down(t, ring.across()).wait_send()

    share.wait_send()
    for n in range(orbitals):
        center(n).wait_send()
    for q in range(chunks):
        cross(q).wait_send()
    spread.drain()
    gather.drain()
    for q in range(chunks):
        across(other, q).wait_recv()
        across(ours, q).wait_send()


def own_kernel(owner_ref, total_ref, out_ref):
    for b in range(total_ref.shape[0]):
        out_ref[b] = jnp.where(owner_ref[b] == lax.axis_index("orb"), total_ref[b], 0.0)


def shards(count, grids, potentials, orbitals, local_pot, shifts, occupation, owner):
    _, blocks, kinds, rows, cells = potentials.shape
    batch = blocks * kinds
    half = batch // PAIR
    orbital_count = orbitals.shape[0]
    planes = rows + 2 * HALO
    pairs = half // (SUB // orbital_count)
    stored = potentials.reshape(PAIR, half, rows, cells)
    vmem = pl.BlockSpec(memory_space=pltpu.VMEM)
    smem = pl.BlockSpec(memory_space=pltpu.SMEM)
    hbm = pl.BlockSpec(memory_space=pl.ANY)
    f32 = jnp.float32
    dma = pltpu.SemaphoreType.DMA
    chunks = half * (rows // HALO)
    slots = pltpu.VMEM((chunks, HALO, cells), f32)
    big = pltpu.VMEM((planes, SUB, cells), f32)
    packed = pltpu.VMEM((planes * SUB, cells), jnp.bfloat16)
    totals = pl.pallas_call(
        functools.partial(respond_kernel, count, grids, kinds),
        out_shape=jax.ShapeDtypeStruct((PAIR, half, rows, cells), f32),
        in_specs=[smem, smem, smem, hbm, hbm, hbm],
        out_specs=vmem,
        scratch_shapes=[
            pltpu.VMEM((half, rows, cells), f32),
            slots,
            slots,
            pltpu.VMEM((half, planes, cells), f32),
            pltpu.VMEM((PAIR * orbital_count, planes, cells), f32),
            pltpu.VMEM((planes, cells), f32),
            pltpu.VMEM((PAIR, 2 * SUB, LANES), f32),
            pltpu.VMEM((half, rows, cells), f32),
            pltpu.VMEM((cells // LANES, pairs * rows * SUB, LANES), f32),
            slots, slots, slots, slots, slots, slots, slots, slots,
            big, big, big, pltpu.VMEM((rows, SUB, cells), f32), big, big,
            packed, packed, packed, packed,
            pltpu.VMEM((planes * SUB, WIDTH), f32),
            pltpu.VMEM((2 * WIDTH, WIDTH), jnp.bfloat16),
            dma((2 + orbital_count,)), dma((2, chunks)), dma((4, chunks)), dma((4, chunks)),
            dma((2, 2, half)), dma((2, 2, 1 + 2 * orbital_count)), dma((2, 1 + orbital_count)),
            dma((2, chunks)),
        ],
        compiler_params=pltpu.CompilerParams(collective_id=0, has_side_effects=True),
        name="respond",
    )(owner, shifts, occupation, stored, orbitals, local_pot)
    response = pl.pallas_call(
        own_kernel,
        out_shape=jax.ShapeDtypeStruct((blocks, kinds, rows, cells), f32),
        in_specs=[smem, vmem],
        out_specs=vmem,
        name="own",
    )(owner, totals.reshape(blocks, kinds, rows, cells))
    return response[None]


def solution(mesh):
    in_specs = (
        P("orb", None, None, "grid", None),
        P("orb", "grid", None),
        P("grid", None),
        P("orb"),
        P("orb"),
        P(),
    )
    out_specs = P("orb", None, None, "grid", None)
    body = functools.partial(shards, mesh.shape["orb"], mesh.shape["grid"])
    return jax.shard_map(body, mesh=mesh, in_specs=in_specs, out_specs=out_specs, check_vma=False)
```

```python
import functools

import jax
import jax.numpy as jnp
from jax import lax
from jax.experimental import pallas as pl
from jax.experimental.pallas import tpu as pltpu
from jax.sharding import PartitionSpec as P

NZ = 32
ITERS = 4
REACH = 2
HALO = REACH * ITERS
KINETIC_DIAG = 3.75
PAIR = 2
MESH = pl.DeviceIdType.MESH


class Ring:
    def __init__(self, count, grids):
        self.count, self.lines, self.grids = count, count // PAIR, grids
        self.me = lax.axis_index("orb")
        self.row = lax.axis_index("grid")
        self.line, self.side = self.me // PAIR, self.me % PAIR
        self.partner = self.line * PAIR + (1 - self.side)

    def at_line(self, line):
        return {"orb": line * PAIR + self.side, "grid": self.row}

    def across(self):
        return {"orb": self.partner, "grid": self.row}

    def up(self):
        return {"orb": self.me, "grid": self.row - 1}

    def down(self):
        return {"orb": self.me, "grid": self.row + 1}


def enter(ring, with_grid):
    barrier = pltpu.get_barrier_semaphore()
    top = ring.lines - 1

    def greet(target):
        pl.semaphore_signal(barrier, inc=1, device_id=target, device_id_type=MESH)

    greet(ring.across())

    @pl.when(ring.line > 0)
    def _():
        greet(ring.at_line(ring.line - 1))

    @pl.when(ring.line < top)
    def _():
        greet(ring.at_line(ring.line + 1))

    peers = 1 + (ring.line + top) // ring.lines + (2 * top - ring.line) // ring.lines
    if with_grid:

        @pl.when(ring.row > 0)
        def _():
            greet(ring.up())

        @pl.when(ring.row < ring.grids - 1)
        def _():
            greet(ring.down())

        last = ring.grids - 1
        peers = peers + (ring.row + last) // ring.grids + (2 * last - ring.row) // ring.grids
    pl.semaphore_wait(barrier, peers)


def send(src, dst, send_sem, recv_sem, target):
    return pltpu.make_async_remote_copy(
        src_ref=src, dst_ref=dst, send_sem=send_sem, recv_sem=recv_sem,
        device_id=target, device_id_type=MESH,
    )


SPREAD_LAG = 4
GATHER_LAG = 3
LANES = 128
WIDTH = 256


class Waves:
    def __init__(self, ring, chunks, lag, buffers, sems):
        self.ring, self.chunks, self.lag, self.sems = ring, chunks, lag, sems
        self.from_left, self.from_right, self.to_right, self.to_left = buffers
        self.has_left, self.has_right = ring.line > 0, ring.line < ring.lines - 1

    def right(self, q, target):
        sems = self.sems
        return send(self.to_right.at[q], self.from_left.at[q], sems.at[0, q], sems.at[1, q], target)

    def left(self, q, target):
        sems = self.sems
        return send(self.to_left.at[q], self.from_right.at[q], sems.at[2, q], sems.at[3, q], target)

    def clear(self):
        @pl.when(jnp.logical_not(self.has_left))
        def _():
            self.from_left[...] = jnp.zeros_like(self.from_left)

        @pl.when(jnp.logical_not(self.has_right))
        def _():
            self.from_right[...] = jnp.zeros_like(self.from_right)

    def begin(self, q, value):
        @pl.when(jnp.logical_not(self.has_left) & self.has_right)
        def _():
            self.to_right[q] = value
            self.right(q, self.ring.at_line(self.ring.line + 1)).start()

        @pl.when(jnp.logical_not(self.has_right) & self.has_left)
        def _():
            self.to_left[q] = value
            self.left(q, self.ring.at_line(self.ring.line - 1)).start()

    def run(self, low, high, prepare, onward, finish):
        ring, lag, line, top = self.ring, self.lag, self.ring.line, self.ring.lines - 1
        beyond = (2 * line) // ring.lines
        late = beyond * line + (1 - beyond) * (top - line)

        def step(s, carry):
            def event(offset, act):
                q = s - offset

                @pl.when((q >= 0) & (q < self.chunks))
                def _():
                    act(q)

            def rightward(q):
                @pl.when(self.has_left)
                def _():
                    self.right(q, ring.across()).wait_recv()

                @pl.when(self.has_left & self.has_right)
                def _():
                    self.to_right[q] = onward(q, self.from_left[q])
                    self.right(q, ring.at_line(line + 1)).start()

            def leftward(q):
                @pl.when(self.has_right)
                def _():
                    self.left(q, ring.across()).wait_recv()

                @pl.when(self.has_left & self.has_right)
                def _():
                    self.to_left[q] = onward(q, self.from_right[q])
                    self.left(q, ring.at_line(line - 1)).start()

            event(0, prepare)
            event(line * lag, rightward)
            event((top - line) * lag, leftward)
            event(late * lag, finish)
            return carry

        lax.fori_loop(low, high, step, 0)

    def steps(self):
        return self.chunks + (self.ring.lines - 1) * self.lag

    def drain(self):
        @pl.when(self.has_right)
        def _():
            for q in range(self.chunks):
                self.right(q, self.ring.across()).wait_send()

        @pl.when(self.has_left)
        def _():
            for q in range(self.chunks):
                self.left(q, self.ring.across()).wait_send()


def chunk_of(ref, q, per, start=0):
    return ref.at[q // per, pl.ds(pl.multiple_of(start + (q % per) * HALO, HALO), HALO)]


def band_matrix(depth, width):
    k = lax.broadcasted_iota(jnp.int32, (depth, width), 0)
    n = lax.broadcasted_iota(jnp.int32, (depth, width), 1) + width // 2
    far_y, far_z = jnp.abs(k // NZ - n // NZ), jnp.abs(k % NZ - n % NZ)
    near = ((far_y == 1) & (far_z == 0)) | ((far_y == 0) & (far_z == 1))
    far = ((far_y == 2) & (far_z == 0)) | ((far_y == 0) & (far_z == 2))
    return jnp.where(near, 16.0, jnp.where(far, -1.0, 0.0)).astype(jnp.bfloat16)


def split(value):
    high = value.astype(jnp.bfloat16)
    return high, (value - high.astype(jnp.float32)).astype(jnp.bfloat16)


class Sweeps:
    def __init__(self, trial, orbs, local, pack, density, scratch):
        self.inverse = scratch[5]
        self.trial, self.orbs, self.local, self.pack, self.density = trial, orbs, local, pack, density
        (
            self.first, self.scale, self.source, self.weighted, self.now_a, self.now_b,
            self.hi_a, self.hi_b, self.lo_a, self.lo_b, self.product, self.band,
        ) = scratch
        self.batch = orbs.shape[0]
        self.planes, self.cells = local.shape

    def start(self):
        self.band[...] = band_matrix(2 * WIDTH, WIDTH)

    def column(self, kind):
        size = self.batch // PAIR
        ours, theirs = self.pack[0, kind * size : (kind + 1) * size], self.pack[1, kind * size : (kind + 1) * size]
        return jnp.broadcast_to(jnp.concatenate([ours, theirs], axis=0)[:, 0:1], (self.batch, self.cells))

    def divide(self, planes, inside):
        shift = self.column(0)
        for p in planes:
            here = jnp.broadcast_to(self.local[p : p + 1, :], (self.batch, self.cells))
            inverse = 1.0 / (KINETIC_DIAG + (here + shift))
            if inside is not None:
                inverse = jnp.where(inside, inverse, 0.0)
            self.inverse[p] = inverse
            self.scale[p] = inverse * (1.0 / 24.0)

    def combine(self, planes, center):
        batch, cells = self.batch, self.cells
        which = lax.broadcasted_iota(jnp.int32, (batch, cells), 0)
        weight = self.column(1) if center else None
        for p in planes:
            orb = jnp.broadcast_to(self.orbs[0, p : p + 1, :], (batch, cells))
            for n in range(1, batch):
                other = jnp.broadcast_to(self.orbs[n, p : p + 1, :], (batch, cells))
                orb = jnp.where(which < n, orb, other)
            self.source[p] = -(orb * self.inverse[p])
            if center:
                self.weighted[p - HALO] = weight * orb

    def run(self, t):
        planes, cells, first, scale = self.planes, self.cells, self.first, self.scale
        batch = self.batch
        for x in range(0, planes, 2):
            values = []
            for p in (x, x + 1):
                value = jnp.broadcast_to(self.trial[t, p : p + 1, :], (batch, cells)) * self.source[p]
                first[p] = value
                values.append(value)
            high, low = split(jnp.concatenate(values, axis=0))
            self.hi_a[x * batch : (x + 2) * batch] = high
            self.lo_a[x * batch : (x + 2) * batch] = low
        current = first
        buffers = ((self.now_a, self.hi_a, self.lo_a), (self.now_b, self.hi_b, self.lo_b))
        product = self.product
        for repeat in range(ITERS):
            hi_in, lo_in = buffers[repeat % 2][1:]
            target, hi_out, lo_out = buffers[(repeat + 1) % 2]
            margin = REACH * (repeat + 1)
            extent = planes - 2 * margin
            for left in range(0, cells, WIDTH):
                a = max(0, left - WIDTH // 2)
                b = min(cells, left + WIDTH + WIDTH // 2)
                k = a - (left - WIDTH // 2)
                weights = self.band[k : k + b - a, :]
                span = slice(margin * batch, (margin + extent) * batch)
                product[0 : extent * batch] = jnp.dot(
                    hi_in[span, a:b], weights, preferred_element_type=jnp.float32
                ) + jnp.dot(lo_in[span, a:b], weights, preferred_element_type=jnp.float32)
                lanes = slice(left, left + WIDTH)
                for x in range(margin, margin + extent, 2):
                    values = []
                    for p in (x, x + 1):
                        near = current[p - 1, :, lanes] + current[p + 1, :, lanes]
                        far = current[p - 2, :, lanes] + current[p + 2, :, lanes]
                        spot = (p - margin) * batch
                        moved = product[spot : spot + batch] + (16.0 * near - far)
                        value = first[p, :, lanes] + scale[p, :, lanes] * moved
                        if repeat == ITERS - 1:
                            where = slice((p - margin) * batch, (p - margin + 1) * batch)
                            term = self.weighted[p - margin, :, lanes] * value
                            for c in range(WIDTH // LANES):
                                block = left // LANES + c
                                self.density[block, where, :] = term[:, c * LANES : (c + 1) * LANES]
                        else:
                            target[p, :, lanes] = value
                            values.append(value)
                    if values:
                        high, low = split(jnp.concatenate(values, axis=0))
                        hi_out[x * batch : (x + 2) * batch, lanes] = high
                        lo_out[x * batch : (x + 2) * batch, lanes] = low
            current = target

    def collect(self, c):
        base = c * HALO * self.batch
        pieces = []
        for block in range(self.cells // LANES):
            total = self.density[block, pl.ds(base, HALO, stride=self.batch), :]
            for n in range(1, self.batch):
                total = total + self.density[block, pl.ds(base + n, HALO, stride=self.batch), :]
            pieces.append(total)
        return jnp.concatenate(pieces, axis=1)


def respond_kernel(
    count, grids, kinds, owner_ref, shift_ref, weight_ref, pot_ref, orb_ref, local_ref, out_ref,
    mine, crossed, merged, trial, orbs, local, pack, part, density,
    s_left, s_right, s_rightward, s_leftward, r_left, r_right, r_rightward, r_leftward,
    first, scale, source, weighted, now_a, now_b, hi_a, hi_b, lo_a, lo_b, product, band,
    load_sems, cross_sems, s_sems, r_sems, halo_sems, edge_sems, pair_sems, side_sems,
):
    ring = Ring(count, grids)
    orbitals, rows, cells = orb_ref.shape
    half = pot_ref.shape[1]
    per = rows // HALO
    chunks = half * per
    last = HALO + rows
    has_up, has_down = ring.row > 0, ring.row < grids - 1
    spread = Waves(ring, chunks, SPREAD_LAG, (s_left, s_right, s_rightward, s_leftward), s_sems)
    gather = Waves(ring, chunks, GATHER_LAG, (r_left, r_right, r_rightward, r_leftward), r_sems)
    sweeps = Sweeps(
        trial, orbs, local, pack, density,
        (first, scale, source, weighted, now_a, now_b, hi_a, hi_b, lo_a, lo_b, product, band),
    )

    def orb_rows(k, n, start, size):
        return orbs.at[k * orbitals + n, pl.ds(start, size)]

    loads = [
        pltpu.make_async_copy(pot_ref.at[ring.side], mine, load_sems.at[0]),
        pltpu.make_async_copy(local_ref, local.at[pl.ds(HALO, rows)], load_sems.at[1]),
    ] + [
        pltpu.make_async_copy(orb_ref.at[n], orb_rows(0, n, HALO, rows), load_sems.at[2 + n])
        for n in range(orbitals)
    ]
    for load in loads:
        load.start()
    for n in range(orbitals):
        pack[0, n] = jnp.full((LANES,), shift_ref[n], jnp.float32)
        pack[0, orbitals + n] = jnp.full((LANES,), weight_ref[n].astype(jnp.float32), jnp.float32)
    spread.clear()
    gather.clear()

    def clear(start):
        orbs[:, start : start + HALO] = jnp.zeros((PAIR * orbitals, HALO, cells), jnp.float32)
        local[start : start + HALO] = jnp.zeros((HALO, cells), jnp.float32)
        trial[:, start : start + HALO] = jnp.zeros((half, HALO, cells), jnp.float32)

    @pl.when(jnp.logical_not(has_up))
    def _():
        clear(0)

    @pl.when(jnp.logical_not(has_down))
    def _():
        clear(last)

    enter(ring, True)

    def cross(q):
        return send(
            chunk_of(pot_ref.at[1 - ring.side], q, per), crossed.at[q],
            cross_sems.at[0, q], cross_sems.at[1, q], ring.across(),
        )

    share = send(pack.at[0], pack.at[1], pair_sems.at[0, orbitals], pair_sems.at[1, orbitals], ring.across())
    share.start()
    for q in range(chunks):
        cross(q).start()

    def center(n):
        return send(
            orb_ref.at[n], orb_rows(1, n, HALO, rows),
            pair_sems.at[0, n], pair_sems.at[1, n], ring.across(),
        )

    for n in range(orbitals):
        center(n).start()

    def edge_up(k, target):
        if k == 0:
            src, dst = local_ref.at[pl.ds(0, HALO)], local.at[pl.ds(last, HALO)]
        elif k <= orbitals:
            src, dst = orb_ref.at[k - 1, pl.ds(0, HALO)], orb_rows(0, k - 1, last, HALO)
        else:
            n = k - 1 - orbitals
            src, dst = orb_rows(1, n, HALO, HALO), orb_rows(1, n, last, HALO)
        return send(src, dst, edge_sems.at[0, 0, k], edge_sems.at[1, 0, k], target)

    def edge_down(k, target):
        if k == 0:
            src, dst = local_ref.at[pl.ds(rows - HALO, HALO)], local.at[pl.ds(0, HALO)]
        elif k <= orbitals:
            src, dst = orb_ref.at[k - 1, pl.ds(rows - HALO, HALO)], orb_rows(0, k - 1, 0, HALO)
        else:
            n = k - 1 - orbitals
            src, dst = orb_rows(1, n, rows, HALO), orb_rows(1, n, 0, HALO)
        return send(src, dst, edge_sems.at[0, 1, k], edge_sems.at[1, 1, k], target)

    own = range(0, 1 + orbitals)
    theirs = range(1 + orbitals, 1 + 2 * orbitals)

    def start_edges(which):
        @pl.when(has_up)
        def _():
            for k in which:
                edge_up(k, ring.up()).start()

        @pl.when(has_down)
        def _():
            for k in which:
                edge_down(k, ring.down()).start()

    def await_edges(which):
        @pl.when(has_up)
        def _():
            for k in which:
                edge_down(k, ring.across()).wait_recv()

        @pl.when(has_down)
        def _():
            for k in which:
                edge_up(k, ring.across()).wait_recv()

    start_edges(own)
    sweeps.start()
    loads[0].wait()

    def owner_of(q):
        return owner_ref[(ring.side * half + q // per) // kinds]

    def halo_up(t, target):
        return send(
            trial.at[t, pl.ds(HALO, HALO)], trial.at[t, pl.ds(last, HALO)],
            halo_sems.at[0, 0, t], halo_sems.at[1, 0, t], target,
        )

    def halo_down(t, target):
        return send(
            trial.at[t, pl.ds(rows, HALO)], trial.at[t, pl.ds(0, HALO)],
            halo_sems.at[0, 1, t], halo_sems.at[1, 1, t], target,
        )

    def merge(q):
        cross(q).wait_recv()
        value = jnp.where(owner_of(q) == ring.partner, crossed[q], chunk_of(mine, q, per)[...])
        merged[q] = value
        spread.begin(q, jnp.where(owner_of(q) // PAIR == ring.line, value, 0.0))

    def select(q, came):
        return jnp.where(owner_of(q) // PAIR == ring.line, merged[q], came)

    def settle(q):
        place = owner_of(q) // PAIR
        other = jnp.where(place < ring.line, s_left[q], s_right[q])
        chunk_of(trial, q, per, HALO)[...] = jnp.where(place == ring.line, merged[q], other)

        @pl.when(has_up & (q % per == 0))
        def _():
            halo_up(q // per, ring.up()).start()

        @pl.when(has_down & (q % per == per - 1))
        def _():
            halo_down(q // per, ring.down()).start()

    first_trial = (ring.lines - 1) * SPREAD_LAG + per
    inner, outer = range(HALO, last), (range(0, HALO), range(last, last + HALO))
    spread.run(0, SPREAD_LAG, merge, select, settle)
    share.wait_recv()
    loads[1].wait()
    sweeps.divide(inner, None)
    spread.run(SPREAD_LAG, first_trial, merge, select, settle)
    for n in range(orbitals):
        center(n).wait_recv()
    start_edges(theirs)
    for load in loads[2:]:
        load.wait()
    sweeps.combine(inner, True)
    await_edges(own)
    sweeps.divide(outer[0], has_up)
    sweeps.divide(outer[1], has_down)
    spread.run(first_trial, first_trial + SPREAD_LAG, merge, select, settle)
    await_edges(theirs)
    sweeps.combine(outer[0], False)
    sweeps.combine(outer[1], False)

    def add(q, came):
        return came + chunk_of(part, q, per)[...]

    ours, other = out_ref.at[ring.side], out_ref.at[1 - ring.side]

    def across(view, q):
        piece = chunk_of(view, q, per)
        return send(piece, piece, side_sems.at[0, q], side_sems.at[1, q], ring.across())

    def finish(q):
        total = r_left[q] + chunk_of(part, q, per)[...] + r_right[q]
        chunk_of(ours, q, per)[...] = total
        across(ours, q).start()

    def item(t, carry):
        @pl.when(has_up)
        def _():
            halo_down(t, ring.across()).wait_recv()

        @pl.when(has_down)
        def _():
            halo_up(t, ring.across()).wait_recv()

        sweeps.run(t)

        @pl.when(t == 0)
        def _():
            spread.run(first_trial + SPREAD_LAG, spread.steps(), merge, select, settle)

        for c in range(per):
            value = sweeps.collect(c)
            part[t, c * HALO : (c + 1) * HALO] = value
            gather.begin(t * per + c, value)
        gather.run((t - 1) * per + 1, t * per + 1, lambda q: None, add, finish)
        return carry

    lax.fori_loop(0, half, item, 0)
    gather.run((half - 1) * per + 1, gather.steps(), lambda q: None, add, finish)

    def sent(which):
        @pl.when(has_up)
        def _():
            for k in which:
                edge_up(k, ring.across()).wait_send()

        @pl.when(has_down)
        def _():
            for k in which:
                edge_down(k, ring.across()).wait_send()

    sent(own)
    sent(theirs)

    @pl.when(has_up)
    def _():
        for t in range(half):
            halo_up(t, ring.across()).wait_send()

    @pl.when(has_down)
    def _():
        for t in range(half):
            halo_down(t, ring.across()).wait_send()

    share.wait_send()
    for n in range(orbitals):
        center(n).wait_send()
    for q in range(chunks):
        cross(q).wait_send()
    spread.drain()
    gather.drain()
    for q in range(chunks):
        across(other, q).wait_recv()
        across(ours, q).wait_send()


def own_kernel(owner_ref, total_ref, out_ref):
    for b in range(total_ref.shape[0]):
        out_ref[b] = jnp.where(owner_ref[b] == lax.axis_index("orb"), total_ref[b], 0.0)


def shards(count, grids, potentials, orbitals, local_pot, shifts, occupation, owner):
    _, blocks, kinds, rows, cells = potentials.shape
    batch = blocks * kinds
    half = batch // PAIR
    orbital_count = orbitals.shape[0]
    planes = rows + 2 * HALO
    wide = PAIR * orbital_count
    stored = potentials.reshape(PAIR, half, rows, cells)
    vmem = pl.BlockSpec(memory_space=pltpu.VMEM)
    smem = pl.BlockSpec(memory_space=pltpu.SMEM)
    hbm = pl.BlockSpec(memory_space=pl.ANY)
    f32 = jnp.float32
    dma = pltpu.SemaphoreType.DMA
    chunks = half * (rows // HALO)
    slots = pltpu.VMEM((chunks, HALO, cells), f32)
    big = pltpu.VMEM((planes, wide, cells), f32)
    packed = pltpu.VMEM((planes * wide, cells), jnp.bfloat16)
    totals = pl.pallas_call(
        functools.partial(respond_kernel, count, grids, kinds),
        out_shape=jax.ShapeDtypeStruct((PAIR, half, rows, cells), f32),
        in_specs=[smem, smem, smem, hbm, hbm, hbm],
        out_specs=vmem,
        scratch_shapes=[
            pltpu.VMEM((half, rows, cells), f32),
            slots,
            slots,
            pltpu.VMEM((half, planes, cells), f32),
            pltpu.VMEM((PAIR * orbital_count, planes, cells), f32),
            pltpu.VMEM((planes, cells), f32),
            pltpu.VMEM((PAIR, 2 * orbital_count, LANES), f32),
            pltpu.VMEM((half, rows, cells), f32),
            pltpu.VMEM((cells // LANES, rows * wide, LANES), f32),
            slots, slots, slots, slots, slots, slots, slots, slots,
            big, big, big, pltpu.VMEM((rows, wide, cells), f32), big, big,
            packed, packed, packed, packed,
            pltpu.VMEM((planes * wide, WIDTH), f32),
            pltpu.VMEM((2 * WIDTH, WIDTH), jnp.bfloat16),
            dma((2 + orbital_count,)), dma((2, chunks)), dma((4, chunks)), dma((4, chunks)),
            dma((2, 2, half)), dma((2, 2, 1 + 2 * orbital_count)), dma((2, 1 + orbital_count)),
            dma((2, chunks)),
        ],
        compiler_params=pltpu.CompilerParams(collective_id=0, has_side_effects=True),
        name="respond",
    )(owner, shifts, occupation, stored, orbitals, local_pot)
    response = pl.pallas_call(
        own_kernel,
        out_shape=jax.ShapeDtypeStruct((blocks, kinds, rows, cells), f32),
        in_specs=[smem, vmem],
        out_specs=vmem,
        name="own",
    )(owner, totals.reshape(blocks, kinds, rows, cells))
    return response[None]


def solution(mesh):
    in_specs = (
        P("orb", None, None, "grid", None),
        P("orb", "grid", None),
        P("grid", None),
        P("orb"),
        P("orb"),
        P(),
    )
    out_specs = P("orb", None, None, "grid", None)
    body = functools.partial(shards, mesh.shape["orb"], mesh.shape["grid"])
    return jax.shard_map(body, mesh=mesh, in_specs=in_specs, out_specs=out_specs, check_vma=False)
```

```python
import functools

import jax
import jax.numpy as jnp
from jax import lax
from jax.experimental import pallas as pl
from jax.experimental.pallas import tpu as pltpu
from jax.sharding import PartitionSpec as P

NZ = 32
ITERS = 4
REACH = 2
HALO = REACH * ITERS
KINETIC_DIAG = 3.75
PAIR = 2
MESH = pl.DeviceIdType.MESH


class Ring:
    def __init__(self, count, grids):
        self.count, self.lines, self.grids = count, count // PAIR, grids
        self.me = lax.axis_index("orb")
        self.row = lax.axis_index("grid")
        self.line, self.side = self.me // PAIR, self.me % PAIR
        self.partner = self.line * PAIR + (1 - self.side)

    def at_line(self, line):
        return {"orb": line * PAIR + self.side, "grid": self.row}

    def across(self):
        return {"orb": self.partner, "grid": self.row}

    def up(self):
        return {"orb": self.me, "grid": self.row - 1}

    def down(self):
        return {"orb": self.me, "grid": self.row + 1}


def enter(ring, with_grid):
    barrier = pltpu.get_barrier_semaphore()
    top = ring.lines - 1

    def greet(target):
        pl.semaphore_signal(barrier, inc=1, device_id=target, device_id_type=MESH)

    greet(ring.across())

    @pl.when(ring.line > 0)
    def _():
        greet(ring.at_line(ring.line - 1))

    @pl.when(ring.line < top)
    def _():
        greet(ring.at_line(ring.line + 1))

    peers = 1 + (ring.line + top) // ring.lines + (2 * top - ring.line) // ring.lines
    if with_grid:

        @pl.when(ring.row > 0)
        def _():
            greet(ring.up())

        @pl.when(ring.row < ring.grids - 1)
        def _():
            greet(ring.down())

        last = ring.grids - 1
        peers = peers + (ring.row + last) // ring.grids + (2 * last - ring.row) // ring.grids
    pl.semaphore_wait(barrier, peers)


def send(src, dst, send_sem, recv_sem, target):
    return pltpu.make_async_remote_copy(
        src_ref=src, dst_ref=dst, send_sem=send_sem, recv_sem=recv_sem,
        device_id=target, device_id_type=MESH,
    )


SPREAD_LAG = 4
FORWARD = 9
GATHER_LAG = 3
LANES = 128
WIDTH = 256


class Waves:
    def __init__(self, ring, chunks, lag, buffers, sems):
        self.ring, self.chunks, self.lag, self.sems = ring, chunks, lag, sems
        self.from_left, self.from_right, self.to_right, self.to_left = buffers
        self.has_left, self.has_right = ring.line > 0, ring.line < ring.lines - 1

    def right(self, q, target):
        sems = self.sems
        return send(self.to_right.at[q], self.from_left.at[q], sems.at[0, q], sems.at[1, q], target)

    def left(self, q, target):
        sems = self.sems
        return send(self.to_left.at[q], self.from_right.at[q], sems.at[2, q], sems.at[3, q], target)

    def clear(self):
        @pl.when(jnp.logical_not(self.has_left))
        def _():
            self.from_left[...] = jnp.zeros_like(self.from_left)

        @pl.when(jnp.logical_not(self.has_right))
        def _():
            self.from_right[...] = jnp.zeros_like(self.from_right)

    def begin(self, q, value):
        @pl.when(jnp.logical_not(self.has_left) & self.has_right)
        def _():
            self.to_right[q] = value
            self.right(q, self.ring.at_line(self.ring.line + 1)).start()

        @pl.when(jnp.logical_not(self.has_right) & self.has_left)
        def _():
            self.to_left[q] = value
            self.left(q, self.ring.at_line(self.ring.line - 1)).start()

    def run(self, low, high, prepare, onward, finish):
        ring, lag, line, top = self.ring, self.lag, self.ring.line, self.ring.lines - 1
        beyond = (2 * line) // ring.lines
        late = beyond * line + (1 - beyond) * (top - line)

        def step(s, carry):
            def event(offset, act):
                q = s - offset

                @pl.when((q >= 0) & (q < self.chunks))
                def _():
                    act(q)

            def rightward(q):
                @pl.when(self.has_left)
                def _():
                    self.right(q, ring.across()).wait_recv()

                @pl.when(self.has_left & self.has_right)
                def _():
                    self.to_right[q] = onward(q, self.from_left[q])
                    self.right(q, ring.at_line(line + 1)).start()

            def leftward(q):
                @pl.when(self.has_right)
                def _():
                    self.left(q, ring.across()).wait_recv()

                @pl.when(self.has_left & self.has_right)
                def _():
                    self.to_left[q] = onward(q, self.from_right[q])
                    self.left(q, ring.at_line(line - 1)).start()

            event(0, prepare)
            event(line * lag, rightward)
            event((top - line) * lag, leftward)
            event(late * lag, finish)
            return carry

        lax.fori_loop(low, high, step, 0)

    def steps(self):
        return self.chunks + (self.ring.lines - 1) * self.lag

    def drain(self):
        @pl.when(self.has_right)
        def _():
            for q in range(self.chunks):
                self.right(q, self.ring.across()).wait_send()

        @pl.when(self.has_left)
        def _():
            for q in range(self.chunks):
                self.left(q, self.ring.across()).wait_send()


def chunk_of(ref, q, per, start=0):
    return ref.at[q // per, pl.ds(pl.multiple_of(start + (q % per) * HALO, HALO), HALO)]


def band_matrix(depth, width):
    k = lax.broadcasted_iota(jnp.int32, (depth, width), 0)
    n = lax.broadcasted_iota(jnp.int32, (depth, width), 1) + width // 2
    far_y, far_z = jnp.abs(k // NZ - n // NZ), jnp.abs(k % NZ - n % NZ)
    near = ((far_y == 1) & (far_z == 0)) | ((far_y == 0) & (far_z == 1))
    far = ((far_y == 2) & (far_z == 0)) | ((far_y == 0) & (far_z == 2))
    return jnp.where(near, 16.0, jnp.where(far, -1.0, 0.0)).astype(jnp.bfloat16)


def split(value):
    high = value.astype(jnp.bfloat16)
    return high, (value - high.astype(jnp.float32)).astype(jnp.bfloat16)


class Sweeps:
    def __init__(self, trial, orbs, local, pack, density, scratch):
        self.inverse = scratch[5]
        self.trial, self.orbs, self.local, self.pack, self.density = trial, orbs, local, pack, density
        (
            self.first, self.scale, self.source, self.weighted, self.now_a, self.now_b,
            self.hi_a, self.hi_b, self.lo_a, self.lo_b, self.product, self.band,
        ) = scratch
        self.batch = orbs.shape[0]
        self.planes, self.cells = local.shape

    def start(self):
        self.band[...] = band_matrix(2 * WIDTH, WIDTH)

    def column(self, kind):
        size = self.batch // PAIR
        ours, theirs = self.pack[0, kind * size : (kind + 1) * size], self.pack[1, kind * size : (kind + 1) * size]
        return jnp.broadcast_to(jnp.concatenate([ours, theirs], axis=0)[:, 0:1], (self.batch, self.cells))

    def divide(self, planes, inside):
        shift = self.column(0)
        for p in planes:
            here = jnp.broadcast_to(self.local[p : p + 1, :], (self.batch, self.cells))
            inverse = 1.0 / (KINETIC_DIAG + (here + shift))
            if inside is not None:
                inverse = jnp.where(inside, inverse, 0.0)
            self.inverse[p] = inverse
            self.scale[p] = inverse * (1.0 / 24.0)

    def combine(self, planes, center):
        batch, cells = self.batch, self.cells
        which = lax.broadcasted_iota(jnp.int32, (batch, cells), 0)
        weight = self.column(1) if center else None
        for p in planes:
            orb = jnp.broadcast_to(self.orbs[0, p : p + 1, :], (batch, cells))
            for n in range(1, batch):
                other = jnp.broadcast_to(self.orbs[n, p : p + 1, :], (batch, cells))
                orb = jnp.where(which < n, orb, other)
            self.source[p] = -(orb * self.inverse[p])
            if center:
                self.weighted[p - HALO] = weight * orb

    def run(self, t):
        planes, cells, first, scale = self.planes, self.cells, self.first, self.scale
        batch = self.batch
        for x in range(0, planes, 2):
            values = []
            for p in (x, x + 1):
                value = jnp.broadcast_to(self.trial[t, p : p + 1, :], (batch, cells)) * self.source[p]
                first[p] = value
                values.append(value)
            high, low = split(jnp.concatenate(values, axis=0))
            self.hi_a[x * batch : (x + 2) * batch] = high
            self.lo_a[x * batch : (x + 2) * batch] = low
        current = first
        buffers = ((self.now_a, self.hi_a, self.lo_a), (self.now_b, self.hi_b, self.lo_b))
        product = self.product
        for repeat in range(ITERS):
            hi_in, lo_in = buffers[repeat % 2][1:]
            target, hi_out, lo_out = buffers[(repeat + 1) % 2]
            margin = REACH * (repeat + 1)
            extent = planes - 2 * margin
            for left in range(0, cells, WIDTH):
                a = max(0, left - WIDTH // 2)
                b = min(cells, left + WIDTH + WIDTH // 2)
                k = a - (left - WIDTH // 2)
                weights = self.band[k : k + b - a, :]
                span = slice(margin * batch, (margin + extent) * batch)
                product[0 : extent * batch] = jnp.dot(
                    hi_in[span, a:b], weights, preferred_element_type=jnp.float32
                ) + jnp.dot(lo_in[span, a:b], weights, preferred_element_type=jnp.float32)
                lanes = slice(left, left + WIDTH)
                for x in range(margin, margin + extent, 2):
                    values = []
                    for p in (x, x + 1):
                        near = current[p - 1, :, lanes] + current[p + 1, :, lanes]
                        far = current[p - 2, :, lanes] + current[p + 2, :, lanes]
                        spot = (p - margin) * batch
                        moved = product[spot : spot + batch] + (16.0 * near - far)
                        value = first[p, :, lanes] + scale[p, :, lanes] * moved
                        if repeat == ITERS - 1:
                            where = slice((p - margin) * batch, (p - margin + 1) * batch)
                            term = self.weighted[p - margin, :, lanes] * value
                            for c in range(WIDTH // LANES):
                                block = left // LANES + c
                                self.density[block, where, :] = term[:, c * LANES : (c + 1) * LANES]
                        else:
                            target[p, :, lanes] = value
                            values.append(value)
                    if values:
                        high, low = split(jnp.concatenate(values, axis=0))
                        hi_out[x * batch : (x + 2) * batch, lanes] = high
                        lo_out[x * batch : (x + 2) * batch, lanes] = low
            current = target

    def collect(self, c):
        base = c * HALO * self.batch
        pieces = []
        for block in range(self.cells // LANES):
            total = self.density[block, pl.ds(base, HALO, stride=self.batch), :]
            for n in range(1, self.batch):
                total = total + self.density[block, pl.ds(base + n, HALO, stride=self.batch), :]
            pieces.append(total)
        return jnp.concatenate(pieces, axis=1)


def respond_kernel(
    count, grids, kinds, owner_ref, shift_ref, weight_ref, pot_ref, orb_ref, local_ref, out_ref,
    mine, crossed, merged, ours, theirs_total, trial, orbs, local, pack, part, density,
    s_left, s_right, s_rightward, s_leftward, r_left, r_right, r_rightward, r_leftward,
    first, scale, source, weighted, now_a, now_b, hi_a, hi_b, lo_a, lo_b, product, band,
    load_sems, cross_sems, s_sems, r_sems, halo_sems, edge_sems, pair_sems, side_sems,
):
    ring = Ring(count, grids)
    orbitals, rows, cells = orb_ref.shape
    half = pot_ref.shape[1]
    per = rows // HALO
    chunks = half * per
    last = HALO + rows
    has_up, has_down = ring.row > 0, ring.row < grids - 1
    spread = Waves(ring, chunks, SPREAD_LAG, (s_left, s_right, s_rightward, s_leftward), s_sems)
    gather = Waves(ring, chunks, GATHER_LAG, (r_left, r_right, r_rightward, r_leftward), r_sems)
    sweeps = Sweeps(
        trial, orbs, local, pack, density,
        (first, scale, source, weighted, now_a, now_b, hi_a, hi_b, lo_a, lo_b, product, band),
    )

    def orb_rows(k, n, start, size):
        return orbs.at[k * orbitals + n, pl.ds(start, size)]

    loads = [
        pltpu.make_async_copy(pot_ref.at[ring.side], mine, load_sems.at[0]),
        pltpu.make_async_copy(local_ref, local.at[pl.ds(HALO, rows)], load_sems.at[1]),
    ] + [
        pltpu.make_async_copy(orb_ref.at[n], orb_rows(0, n, HALO, rows), load_sems.at[2 + n])
        for n in range(orbitals)
    ]
    for load in loads:
        load.start()
    for n in range(orbitals):
        pack[0, n] = jnp.full((LANES,), shift_ref[n], jnp.float32)
        pack[0, orbitals + n] = jnp.full((LANES,), weight_ref[n].astype(jnp.float32), jnp.float32)
    spread.clear()
    gather.clear()

    def clear(start):
        orbs[:, start : start + HALO] = jnp.zeros((PAIR * orbitals, HALO, cells), jnp.float32)
        local[start : start + HALO] = jnp.zeros((HALO, cells), jnp.float32)
        trial[:, start : start + HALO] = jnp.zeros((half, HALO, cells), jnp.float32)

    @pl.when(jnp.logical_not(has_up))
    def _():
        clear(0)

    @pl.when(jnp.logical_not(has_down))
    def _():
        clear(last)

    enter(ring, True)

    def cross(q):
        return send(
            chunk_of(pot_ref.at[1 - ring.side], q, per), crossed.at[q],
            cross_sems.at[0, q], cross_sems.at[1, q], ring.across(),
        )

    share = send(pack.at[0], pack.at[1], pair_sems.at[0, orbitals], pair_sems.at[1, orbitals], ring.across())
    share.start()
    for q in range(chunks):
        cross(q).start()

    def center(n):
        return send(
            orb_ref.at[n], orb_rows(1, n, HALO, rows),
            pair_sems.at[0, n], pair_sems.at[1, n], ring.across(),
        )

    for n in range(orbitals):
        center(n).start()

    def edge_up(k, target):
        if k == 0:
            src, dst = local_ref.at[pl.ds(0, HALO)], local.at[pl.ds(last, HALO)]
        elif k <= orbitals:
            src, dst = orb_ref.at[k - 1, pl.ds(0, HALO)], orb_rows(0, k - 1, last, HALO)
        else:
            n = k - 1 - orbitals
            src, dst = orb_rows(1, n, HALO, HALO), orb_rows(1, n, last, HALO)
        return send(src, dst, edge_sems.at[0, 0, k], edge_sems.at[1, 0, k], target)

    def edge_down(k, target):
        if k == 0:
            src, dst = local_ref.at[pl.ds(rows - HALO, HALO)], local.at[pl.ds(0, HALO)]
        elif k <= orbitals:
            src, dst = orb_ref.at[k - 1, pl.ds(rows - HALO, HALO)], orb_rows(0, k - 1, 0, HALO)
        else:
            n = k - 1 - orbitals
            src, dst = orb_rows(1, n, rows, HALO), orb_rows(1, n, 0, HALO)
        return send(src, dst, edge_sems.at[0, 1, k], edge_sems.at[1, 1, k], target)

    own = range(0, 1 + orbitals)
    theirs = range(1 + orbitals, 1 + 2 * orbitals)

    def start_edges(which):
        @pl.when(has_up)
        def _():
            for k in which:
                edge_up(k, ring.up()).start()

        @pl.when(has_down)
        def _():
            for k in which:
                edge_down(k, ring.down()).start()

    def await_edges(which):
        @pl.when(has_up)
        def _():
            for k in which:
                edge_down(k, ring.across()).wait_recv()

        @pl.when(has_down)
        def _():
            for k in which:
                edge_up(k, ring.across()).wait_recv()

    start_edges(own)
    sweeps.start()
    loads[0].wait()

    def owner_of(q):
        return owner_ref[(ring.side * half + q // per) // kinds]

    def halo_up(t, target):
        return send(
            trial.at[t, pl.ds(HALO, HALO)], trial.at[t, pl.ds(last, HALO)],
            halo_sems.at[0, 0, t], halo_sems.at[1, 0, t], target,
        )

    def halo_down(t, target):
        return send(
            trial.at[t, pl.ds(rows, HALO)], trial.at[t, pl.ds(0, HALO)],
            halo_sems.at[0, 1, t], halo_sems.at[1, 1, t], target,
        )

    def merge(q):
        cross(q).wait_recv()
        value = jnp.where(owner_of(q) == ring.partner, crossed[q], chunk_of(mine, q, per)[...])
        merged[q] = value
        spread.begin(q, jnp.where(owner_of(q) // PAIR == ring.line, value, 0.0))

    def select(q, came):
        return jnp.where(owner_of(q) // PAIR == ring.line, merged[q], came)

    def settle(q):
        place = owner_of(q) // PAIR
        other = jnp.where(place < ring.line, s_left[q], s_right[q])
        chunk_of(trial, q, per, HALO)[...] = jnp.where(place == ring.line, merged[q], other)

        @pl.when(has_up & (q % per == 0))
        def _():
            halo_up(q // per, ring.up()).start()

        @pl.when(has_down & (q % per == per - 1))
        def _():
            halo_down(q // per, ring.down()).start()

    inner, outer = range(HALO, last), (range(0, HALO), range(last, last + HALO))
    spread.run(0, SPREAD_LAG, merge, select, settle)
    share.wait_recv()
    loads[1].wait()
    sweeps.divide(inner, None)
    spread.run(SPREAD_LAG, FORWARD, merge, select, settle)
    for n in range(orbitals):
        center(n).wait_recv()
        start_edges([theirs[n]])
        spread.run(FORWARD + 2 * n, FORWARD + 2 * n + 2, merge, select, settle)
    first_trial = FORWARD + 2 * orbitals
    for load in loads[2:]:
        load.wait()
    sweeps.combine(inner, True)
    await_edges(own)
    sweeps.divide(outer[0], has_up)
    sweeps.divide(outer[1], has_down)
    begin = max((ring.lines - 1) * SPREAD_LAG + per + SPREAD_LAG, first_trial)
    spread.run(first_trial, begin, merge, select, settle)
    await_edges(theirs)
    sweeps.combine(outer[0], False)
    sweeps.combine(outer[1], False)

    def add(q, came):
        return came + chunk_of(part, q, per)[...]

    def across(q):
        return send(
            ours.at[q], theirs_total.at[q], side_sems.at[0, q], side_sems.at[1, q], ring.across()
        )

    def keep(side, q, value):
        owned = owner_ref[(side * half + q // per) // kinds] == ring.me
        chunk_of(out_ref.at[side], q, per)[...] = jnp.where(owned, value, 0.0)

    def finish(q):
        total = r_left[q] + chunk_of(part, q, per)[...] + r_right[q]
        ours[q] = total
        across(q).start()
        keep(ring.side, q, total)

    def item(t, carry):
        @pl.when(has_up)
        def _():
            halo_down(t, ring.across()).wait_recv()

        @pl.when(has_down)
        def _():
            halo_up(t, ring.across()).wait_recv()

        sweeps.run(t)

        @pl.when(t == 0)
        def _():
            spread.run(begin, spread.steps(), merge, select, settle)

        for c in range(per):
            value = sweeps.collect(c)
            part[t, c * HALO : (c + 1) * HALO] = value
            gather.begin(t * per + c, value)
        gather.run((t - 1) * per + 1, t * per + 1, lambda q: None, add, finish)
        return carry

    lax.fori_loop(0, half, item, 0)
    gather.run((half - 1) * per + 1, gather.steps(), lambda q: None, add, finish)

    def sent(which):
        @pl.when(has_up)
        def _():
            for k in which:
                edge_up(k, ring.across()).wait_send()

        @pl.when(has_down)
        def _():
            for k in which:
                edge_down(k, ring.across()).wait_send()

    sent(own)
    sent(theirs)

    @pl.when(has_up)
    def _():
        for t in range(half):
            halo_up(t, ring.across()).wait_send()

    @pl.when(has_down)
    def _():
        for t in range(half):
            halo_down(t, ring.across()).wait_send()

    share.wait_send()
    for n in range(orbitals):
        center(n).wait_send()
    for q in range(chunks):
        cross(q).wait_send()
    spread.drain()
    gather.drain()
    for q in range(chunks):
        across(q).wait_recv()
        keep(1 - ring.side, q, theirs_total[q])
        across(q).wait_send()


def shards(count, grids, potentials, orbitals, local_pot, shifts, occupation, owner):
    _, blocks, kinds, rows, cells = potentials.shape
    batch = blocks * kinds
    half = batch // PAIR
    orbital_count = orbitals.shape[0]
    planes = rows + 2 * HALO
    wide = PAIR * orbital_count
    stored = potentials.reshape(PAIR, half, rows, cells)
    vmem = pl.BlockSpec(memory_space=pltpu.VMEM)
    smem = pl.BlockSpec(memory_space=pltpu.SMEM)
    hbm = pl.BlockSpec(memory_space=pl.ANY)
    f32 = jnp.float32
    dma = pltpu.SemaphoreType.DMA
    chunks = half * (rows // HALO)
    slots = pltpu.VMEM((chunks, HALO, cells), f32)
    big = pltpu.VMEM((planes, wide, cells), f32)
    packed = pltpu.VMEM((planes * wide, cells), jnp.bfloat16)
    response = pl.pallas_call(
        functools.partial(respond_kernel, count, grids, kinds),
        out_shape=pltpu.VMEM((PAIR, half, rows, cells), f32),
        in_specs=[smem, smem, smem, hbm, hbm, hbm],
        out_specs=vmem,
        scratch_shapes=[
            pltpu.VMEM((half, rows, cells), f32),
            slots, slots, slots, slots,
            pltpu.VMEM((half, planes, cells), f32),
            pltpu.VMEM((PAIR * orbital_count, planes, cells), f32),
            pltpu.VMEM((planes, cells), f32),
            pltpu.VMEM((PAIR, 2 * orbital_count, LANES), f32),
            pltpu.VMEM((half, rows, cells), f32),
            pltpu.VMEM((cells // LANES, rows * wide, LANES), f32),
            slots, slots, slots, slots, slots, slots, slots, slots,
            big, big, big, pltpu.VMEM((rows, wide, cells), f32), big, big,
            packed, packed, packed, packed,
            pltpu.VMEM((planes * wide, WIDTH), f32),
            pltpu.VMEM((2 * WIDTH, WIDTH), jnp.bfloat16),
            dma((2 + orbital_count,)), dma((2, chunks)), dma((4, chunks)), dma((4, chunks)),
            dma((2, 2, half)), dma((2, 2, 1 + 2 * orbital_count)), dma((2, 1 + orbital_count)),
            dma((2, chunks)),
        ],
        compiler_params=pltpu.CompilerParams(collective_id=0, has_side_effects=True),
        name="respond",
    )(owner, shifts, occupation, stored, orbitals, local_pot)
    return response.reshape(1, blocks, kinds, rows, cells)


def solution(mesh):
    in_specs = (
        P("orb", None, None, "grid", None),
        P("orb", "grid", None),
        P("grid", None),
        P("orb"),
        P("orb"),
        P(),
    )
    out_specs = P("orb", None, None, "grid", None)
    body = functools.partial(shards, mesh.shape["orb"], mesh.shape["grid"])
    return jax.shard_map(body, mesh=mesh, in_specs=in_specs, out_specs=out_specs, check_vma=False)
```

```python
import functools

import jax
import jax.numpy as jnp
from jax import lax
from jax.experimental import pallas as pl
from jax.experimental.pallas import tpu as pltpu
from jax.sharding import PartitionSpec as P

NZ = 32
ITERS = 4
REACH = 2
HALO = REACH * ITERS
KINETIC_DIAG = 3.75
PAIR = 2
MESH = pl.DeviceIdType.MESH


class Ring:
    def __init__(self, count, grids):
        self.count, self.lines, self.grids = count, count // PAIR, grids
        self.me = lax.axis_index("orb")
        self.row = lax.axis_index("grid")
        self.line, self.side = self.me // PAIR, self.me % PAIR
        self.partner = self.line * PAIR + (1 - self.side)

    def at_line(self, line):
        return {"orb": line * PAIR + self.side, "grid": self.row}

    def across(self):
        return {"orb": self.partner, "grid": self.row}

    def up(self):
        return {"orb": self.me, "grid": self.row - 1}

    def down(self):
        return {"orb": self.me, "grid": self.row + 1}


def greet_peers(ring):
    barrier = pltpu.get_barrier_semaphore()
    top = ring.lines - 1

    def greet(target):
        pl.semaphore_signal(barrier, inc=1, device_id=target, device_id_type=MESH)

    greet(ring.across())

    @pl.when(ring.line > 0)
    def _():
        greet(ring.at_line(ring.line - 1))

    @pl.when(ring.line < top)
    def _():
        greet(ring.at_line(ring.line + 1))

    peers = 1 + (ring.line + top) // ring.lines + (2 * top - ring.line) // ring.lines
    @pl.when(ring.row > 0)
    def _():
        greet(ring.up())

    @pl.when(ring.row < ring.grids - 1)
    def _():
        greet(ring.down())

    last = ring.grids - 1
    peers = peers + (ring.row + last) // ring.grids + (2 * last - ring.row) // ring.grids
    return barrier, peers


def send(src, dst, send_sem, recv_sem, target):
    return pltpu.make_async_remote_copy(
        src_ref=src, dst_ref=dst, send_sem=send_sem, recv_sem=recv_sem,
        device_id=target, device_id_type=MESH,
    )


SPLIT = 1
SPREAD_LAG = 4
FORWARD = 8
FORWARD_STEP = 2
GATHER_LAG = 4
LANES = 128
WIDTH = 256


class Waves:
    def __init__(self, ring, chunks, lag, buffers, sems):
        self.ring, self.chunks, self.lag, self.sems = ring, chunks, lag, sems
        self.from_left, self.from_right, self.to_right, self.to_left = buffers
        self.has_left, self.has_right = ring.line > 0, ring.line < ring.lines - 1

    def right(self, q, target):
        sems = self.sems
        return send(self.to_right.at[q], self.from_left.at[q], sems.at[0, q], sems.at[1, q], target)

    def left(self, q, target):
        sems = self.sems
        return send(self.to_left.at[q], self.from_right.at[q], sems.at[2, q], sems.at[3, q], target)

    def clear(self):
        @pl.when(jnp.logical_not(self.has_left))
        def _():
            self.from_left[...] = jnp.zeros_like(self.from_left)

        @pl.when(jnp.logical_not(self.has_right))
        def _():
            self.from_right[...] = jnp.zeros_like(self.from_right)

    def begin(self, q, value):
        @pl.when(jnp.logical_not(self.has_left) & self.has_right)
        def _():
            self.to_right[q] = value
            self.right(q, self.ring.at_line(self.ring.line + 1)).start()

        @pl.when(jnp.logical_not(self.has_right) & self.has_left)
        def _():
            self.to_left[q] = value
            self.left(q, self.ring.at_line(self.ring.line - 1)).start()

    def run(self, low, high, prepare, onward, finish):
        ring, lag, line, top = self.ring, self.lag, self.ring.line, self.ring.lines - 1
        beyond = (2 * line) // ring.lines
        late = beyond * line + (1 - beyond) * (top - line)

        def step(s, carry):
            def event(offset, act):
                q = s - offset

                @pl.when((q >= 0) & (q < self.chunks))
                def _():
                    act(q)

            def rightward(q):
                @pl.when(self.has_left)
                def _():
                    self.right(q, ring.across()).wait_recv()

                @pl.when(self.has_left & self.has_right)
                def _():
                    self.to_right[q] = onward(q, self.from_left[q])
                    self.right(q, ring.at_line(line + 1)).start()

            def leftward(q):
                @pl.when(self.has_right)
                def _():
                    self.left(q, ring.across()).wait_recv()

                @pl.when(self.has_left & self.has_right)
                def _():
                    self.to_left[q] = onward(q, self.from_right[q])
                    self.left(q, ring.at_line(line - 1)).start()

            event(0, prepare)
            event(line * lag, rightward)
            event((top - line) * lag, leftward)
            event(late * lag, finish)
            return carry

        lax.fori_loop(low, high, step, 0)

    def steps(self):
        return self.chunks + (self.ring.lines - 1) * self.lag

    def drain(self):
        @pl.when(self.has_right)
        def _():
            for q in range(self.chunks):
                self.right(q, self.ring.across()).wait_send()

        @pl.when(self.has_left)
        def _():
            for q in range(self.chunks):
                self.left(q, self.ring.across()).wait_send()


def chunk_of(ref, q, per, start=0):
    width = ref.shape[-1] // SPLIT
    piece = q % per
    rows = pl.ds(pl.multiple_of(start + piece // SPLIT * HALO, HALO), HALO)
    return ref.at[q // per, rows, pl.ds(pl.multiple_of(piece % SPLIT * width, LANES), width)]


def band_matrix(depth, width):
    k = lax.broadcasted_iota(jnp.int32, (depth, width), 0)
    n = lax.broadcasted_iota(jnp.int32, (depth, width), 1) + width // 2
    far_y, far_z = jnp.abs(k // NZ - n // NZ), jnp.abs(k % NZ - n % NZ)
    near = ((far_y == 1) & (far_z == 0)) | ((far_y == 0) & (far_z == 1))
    far = ((far_y == 2) & (far_z == 0)) | ((far_y == 0) & (far_z == 2))
    return jnp.where(near, 16.0, jnp.where(far, -1.0, 0.0)).astype(jnp.bfloat16)


def split(value):
    high = value.astype(jnp.bfloat16)
    return high, (value - high.astype(jnp.float32)).astype(jnp.bfloat16)


class Sweeps:
    def __init__(self, trial, orbs, local, pack, density, scratch):
        self.inverse = scratch[5]
        self.trial, self.orbs, self.local, self.pack, self.density = trial, orbs, local, pack, density
        (
            self.first, self.scale, self.source, self.weighted, self.now_a, self.now_b,
            self.hi_a, self.hi_b, self.lo_a, self.lo_b, self.product, self.band,
        ) = scratch
        self.batch = orbs.shape[0]
        self.planes, self.cells = local.shape

    def start(self):
        self.band[...] = band_matrix(2 * WIDTH, WIDTH)

    def column(self, kind):
        size = self.batch // PAIR
        ours, theirs = self.pack[0, kind * size : (kind + 1) * size], self.pack[1, kind * size : (kind + 1) * size]
        return jnp.broadcast_to(jnp.concatenate([ours, theirs], axis=0)[:, 0:1], (self.batch, self.cells))

    def divide(self, planes, inside):
        shift = self.column(0)
        for p in planes:
            here = jnp.broadcast_to(self.local[p : p + 1, :], (self.batch, self.cells))
            inverse = 1.0 / (KINETIC_DIAG + (here + shift))
            if inside is not None:
                inverse = jnp.where(inside, inverse, 0.0)
            self.inverse[p] = inverse
            self.scale[p] = inverse * (1.0 / 24.0)

    def combine(self, planes, center):
        batch, cells = self.batch, self.cells
        which = lax.broadcasted_iota(jnp.int32, (batch, cells), 0)
        weight = self.column(1) if center else None
        for p in planes:
            orb = jnp.broadcast_to(self.orbs[0, p : p + 1, :], (batch, cells))
            for n in range(1, batch):
                other = jnp.broadcast_to(self.orbs[n, p : p + 1, :], (batch, cells))
                orb = jnp.where(which < n, orb, other)
            self.source[p] = -(orb * self.inverse[p])
            if center:
                self.weighted[p - HALO] = weight * orb

    def run(self, t):
        planes, cells, first, scale = self.planes, self.cells, self.first, self.scale
        batch = self.batch
        for x in range(0, planes, 2):
            values = []
            for p in (x, x + 1):
                value = jnp.broadcast_to(self.trial[t, p : p + 1, :], (batch, cells)) * self.source[p]
                first[p] = value
                values.append(value)
            high, low = split(jnp.concatenate(values, axis=0))
            self.hi_a[x * batch : (x + 2) * batch] = high
            self.lo_a[x * batch : (x + 2) * batch] = low
        current = first
        buffers = ((self.now_a, self.hi_a, self.lo_a), (self.now_b, self.hi_b, self.lo_b))
        product = self.product
        for repeat in range(ITERS):
            hi_in, lo_in = buffers[repeat % 2][1:]
            target, hi_out, lo_out = buffers[(repeat + 1) % 2]
            margin = REACH * (repeat + 1)
            extent = planes - 2 * margin
            for left in range(0, cells, WIDTH):
                a = max(0, left - WIDTH // 2)
                b = min(cells, left + WIDTH + WIDTH // 2)
                k = a - (left - WIDTH // 2)
                weights = self.band[k : k + b - a, :]
                span = slice(margin * batch, (margin + extent) * batch)
                product[0 : extent * batch] = jnp.dot(
                    hi_in[span, a:b], weights, preferred_element_type=jnp.float32
                ) + jnp.dot(lo_in[span, a:b], weights, preferred_element_type=jnp.float32)
                lanes = slice(left, left + WIDTH)
                for x in range(margin, margin + extent, 2):
                    values = []
                    for p in (x, x + 1):
                        near = current[p - 1, :, lanes] + current[p + 1, :, lanes]
                        far = current[p - 2, :, lanes] + current[p + 2, :, lanes]
                        spot = (p - margin) * batch
                        moved = product[spot : spot + batch] + (16.0 * near - far)
                        value = first[p, :, lanes] + scale[p, :, lanes] * moved
                        if repeat == ITERS - 1:
                            where = slice((p - margin) * batch, (p - margin + 1) * batch)
                            term = self.weighted[p - margin, :, lanes] * value
                            for c in range(WIDTH // LANES):
                                block = left // LANES + c
                                self.density[block, where, :] = term[:, c * LANES : (c + 1) * LANES]
                        else:
                            target[p, :, lanes] = value
                            values.append(value)
                    if values:
                        high, low = split(jnp.concatenate(values, axis=0))
                        hi_out[x * batch : (x + 2) * batch, lanes] = high
                        lo_out[x * batch : (x + 2) * batch, lanes] = low
            current = target

    def collect(self, c):
        base = c * HALO * self.batch
        pieces = []
        for block in range(self.cells // LANES):
            total = self.density[block, pl.ds(base, HALO, stride=self.batch), :]
            for n in range(1, self.batch):
                total = total + self.density[block, pl.ds(base + n, HALO, stride=self.batch), :]
            pieces.append(total)
        return jnp.concatenate(pieces, axis=1)


def respond_kernel(
    count, grids, kinds, owner_hbm, shift_hbm, weight_hbm, pot_ref, orb_ref, local_ref, out_ref,
    owner_ref, shift_ref, weight_ref, mine, crossed, merged, ours, theirs_total, trial, orbs, local, pack, part, density,
    s_left, s_right, s_rightward, s_leftward, r_left, r_right, r_rightward, r_leftward,
    first, scale, source, weighted, now_a, now_b, hi_a, hi_b, lo_a, lo_b, product, band,
    scalar_sems, load_sems, cross_sems, s_sems, r_sems, halo_sems, edge_sems, pair_sems, side_sems,
):
    ring = Ring(count, grids)
    orbitals, rows, cells = orb_ref.shape
    half = pot_ref.shape[1]
    per = rows // HALO * SPLIT
    chunks = half * per
    last = HALO + rows
    has_up, has_down = ring.row > 0, ring.row < grids - 1
    spread = Waves(ring, chunks, SPREAD_LAG, (s_left, s_right, s_rightward, s_leftward), s_sems)
    gather = Waves(ring, chunks, GATHER_LAG, (r_left, r_right, r_rightward, r_leftward), r_sems)
    sweeps = Sweeps(
        trial, orbs, local, pack, density,
        (first, scale, source, weighted, now_a, now_b, hi_a, hi_b, lo_a, lo_b, product, band),
    )

    def orb_rows(k, n, start, size):
        return orbs.at[k * orbitals + n, pl.ds(start, size)]

    barrier, peers = greet_peers(ring)
    loads = [
        pltpu.make_async_copy(pot_ref.at[ring.side], mine, load_sems.at[0]),
        pltpu.make_async_copy(local_ref, local.at[pl.ds(HALO, rows)], load_sems.at[1]),
    ] + [
        pltpu.make_async_copy(orb_ref.at[n], orb_rows(0, n, HALO, rows), load_sems.at[2 + n])
        for n in range(orbitals)
    ]
    scalars = [
        pltpu.make_async_copy(src, dst, scalar_sems.at[i])
        for i, (src, dst) in enumerate(
            [(shift_hbm, shift_ref), (weight_hbm, weight_ref), (owner_hbm, owner_ref)]
        )
    ]
    for load in scalars + loads:
        load.start()
    for load in scalars:
        load.wait()
    for n in range(orbitals):
        pack[0, n] = jnp.full((LANES,), shift_ref[n], jnp.float32)
        pack[0, orbitals + n] = jnp.full((LANES,), weight_ref[n].astype(jnp.float32), jnp.float32)
    pl.semaphore_wait(barrier, peers)

    def cross(q):
        return send(
            chunk_of(pot_ref.at[1 - ring.side], q, per), crossed.at[q],
            cross_sems.at[0, q], cross_sems.at[1, q], ring.across(),
        )

    share = send(pack.at[0], pack.at[1], pair_sems.at[0, orbitals], pair_sems.at[1, orbitals], ring.across())
    share.start()
    for q in range(chunks):
        cross(q).start()

    def center(n):
        return send(
            orb_ref.at[n], orb_rows(1, n, HALO, rows),
            pair_sems.at[0, n], pair_sems.at[1, n], ring.across(),
        )

    for n in range(orbitals):
        center(n).start()

    def edge_up(k, target):
        if k == 0:
            src, dst = local_ref.at[pl.ds(0, HALO)], local.at[pl.ds(last, HALO)]
        elif k <= orbitals:
            src, dst = orb_ref.at[k - 1, pl.ds(0, HALO)], orb_rows(0, k - 1, last, HALO)
        else:
            n = k - 1 - orbitals
            src, dst = orb_rows(1, n, HALO, HALO), orb_rows(1, n, last, HALO)
        return send(src, dst, edge_sems.at[0, 0, k], edge_sems.at[1, 0, k], target)

    def edge_down(k, target):
        if k == 0:
            src, dst = local_ref.at[pl.ds(rows - HALO, HALO)], local.at[pl.ds(0, HALO)]
        elif k <= orbitals:
            src, dst = orb_ref.at[k - 1, pl.ds(rows - HALO, HALO)], orb_rows(0, k - 1, 0, HALO)
        else:
            n = k - 1 - orbitals
            src, dst = orb_rows(1, n, rows, HALO), orb_rows(1, n, 0, HALO)
        return send(src, dst, edge_sems.at[0, 1, k], edge_sems.at[1, 1, k], target)

    own = range(0, 1 + orbitals)
    theirs = range(1 + orbitals, 1 + 2 * orbitals)

    def start_edges(which):
        @pl.when(has_up)
        def _():
            for k in which:
                edge_up(k, ring.up()).start()

        @pl.when(has_down)
        def _():
            for k in which:
                edge_down(k, ring.down()).start()

    def await_edges(which):
        @pl.when(has_up)
        def _():
            for k in which:
                edge_down(k, ring.across()).wait_recv()

        @pl.when(has_down)
        def _():
            for k in which:
                edge_up(k, ring.across()).wait_recv()

    start_edges(own)
    gather.clear()

    def clear(start):
        orbs[:, start : start + HALO] = jnp.zeros((PAIR * orbitals, HALO, cells), jnp.float32)
        local[start : start + HALO] = jnp.zeros((HALO, cells), jnp.float32)
        trial[:, start : start + HALO] = jnp.zeros((half, HALO, cells), jnp.float32)

    @pl.when(jnp.logical_not(has_up))
    def _():
        clear(0)

    @pl.when(jnp.logical_not(has_down))
    def _():
        clear(last)

    sweeps.start()
    loads[0].wait()

    def owner_of(q):
        return owner_ref[(ring.side * half + q // per) // kinds]

    def halo_up(t, target):
        return send(
            trial.at[t, pl.ds(HALO, HALO)], trial.at[t, pl.ds(last, HALO)],
            halo_sems.at[0, 0, t], halo_sems.at[1, 0, t], target,
        )

    def halo_down(t, target):
        return send(
            trial.at[t, pl.ds(rows, HALO)], trial.at[t, pl.ds(0, HALO)],
            halo_sems.at[0, 1, t], halo_sems.at[1, 1, t], target,
        )

    def merge(q):
        cross(q).wait_recv()
        value = jnp.where(owner_of(q) == ring.partner, crossed[q], chunk_of(mine, q, per)[...])
        merged[q] = value
        spread.begin(q, jnp.where(owner_of(q) // PAIR == ring.line, value, 0.0))

    def select(q, came):
        return jnp.where(owner_of(q) // PAIR == ring.line, merged[q], came)

    def settle(q):
        place = owner_of(q) // PAIR
        other = jnp.where(place < ring.line, s_left[q], s_right[q])
        chunk_of(trial, q, per, HALO)[...] = jnp.where(place == ring.line, merged[q], other)

        @pl.when(has_up & (q % per == SPLIT - 1))
        def _():
            halo_up(q // per, ring.up()).start()

        @pl.when(has_down & (q % per == per - 1))
        def _():
            halo_down(q // per, ring.down()).start()

    inner, outer = range(HALO, last), (range(0, HALO), range(last, last + HALO))
    spread.run(0, SPREAD_LAG, merge, select, settle)
    share.wait_recv()
    loads[1].wait()
    sweeps.divide(inner, None)
    spread.run(SPREAD_LAG, FORWARD, merge, select, settle)
    for n in range(orbitals):
        center(n).wait_recv()
        start_edges([theirs[n]])
        spread.run(FORWARD + FORWARD_STEP * n, FORWARD + FORWARD_STEP * (n + 1), merge, select, settle)
    first_trial = FORWARD + FORWARD_STEP * orbitals
    for load in loads[2:]:
        load.wait()
    sweeps.combine(inner, True)
    await_edges(own)
    sweeps.divide(outer[0], has_up)
    sweeps.divide(outer[1], has_down)
    begin = max((ring.lines - 1) * SPREAD_LAG + per + SPREAD_LAG, first_trial)
    spread.run(first_trial, begin, merge, select, settle)
    await_edges(theirs)
    sweeps.combine(outer[0], False)
    sweeps.combine(outer[1], False)

    def add(q, came):
        return came + chunk_of(part, q, per)[...]

    def across(q):
        return send(
            ours.at[q], theirs_total.at[q], side_sems.at[0, q], side_sems.at[1, q], ring.across()
        )

    def keep(side, q, value):
        owned = owner_ref[(side * half + q // per) // kinds] == ring.me
        chunk_of(out_ref.at[side], q, per)[...] = jnp.where(owned, value, 0.0)

    def finish(q):
        total = r_left[q] + chunk_of(part, q, per)[...] + r_right[q]
        ours[q] = total
        across(q).start()
        keep(ring.side, q, total)

    def item(t, carry):
        @pl.when(has_up)
        def _():
            halo_down(t, ring.across()).wait_recv()

        @pl.when(has_down)
        def _():
            halo_up(t, ring.across()).wait_recv()

        sweeps.run(t)

        @pl.when(t == 0)
        def _():
            spread.run(begin, spread.steps(), merge, select, settle)

        for c in range(per // SPLIT):
            value = sweeps.collect(c)
            part[t, c * HALO : (c + 1) * HALO] = value
            width = cells // SPLIT
            for j in range(SPLIT):
                gather.begin(t * per + c * SPLIT + j, value[:, j * width : (j + 1) * width])
        gather.run((t - 1) * per + 1, t * per + 1, lambda q: None, add, finish)
        return carry

    lax.fori_loop(0, half, item, 0)
    gather.run((half - 1) * per + 1, gather.steps(), lambda q: None, add, finish)

    def sent(which):
        @pl.when(has_up)
        def _():
            for k in which:
                edge_up(k, ring.across()).wait_send()

        @pl.when(has_down)
        def _():
            for k in which:
                edge_down(k, ring.across()).wait_send()

    sent(own)
    sent(theirs)

    @pl.when(has_up)
    def _():
        for t in range(half):
            halo_up(t, ring.across()).wait_send()

    @pl.when(has_down)
    def _():
        for t in range(half):
            halo_down(t, ring.across()).wait_send()

    share.wait_send()
    for n in range(orbitals):
        center(n).wait_send()
    for q in range(chunks):
        cross(q).wait_send()
    spread.drain()
    gather.drain()
    for q in range(chunks):
        across(q).wait_recv()
        keep(1 - ring.side, q, theirs_total[q])
        across(q).wait_send()


def shards(count, grids, potentials, orbitals, local_pot, shifts, occupation, owner):
    _, blocks, kinds, rows, cells = potentials.shape
    batch = blocks * kinds
    half = batch // PAIR
    orbital_count = orbitals.shape[0]
    planes = rows + 2 * HALO
    wide = PAIR * orbital_count
    stored = potentials.reshape(PAIR, half, rows, cells)
    vmem = pl.BlockSpec(memory_space=pltpu.VMEM)
    hbm = pl.BlockSpec(memory_space=pl.ANY)
    f32 = jnp.float32
    dma = pltpu.SemaphoreType.DMA
    chunks = half * (rows // HALO) * SPLIT
    slots = pltpu.VMEM((chunks, HALO, cells // SPLIT), f32)
    big = pltpu.VMEM((planes, wide, cells), f32)
    packed = pltpu.VMEM((planes * wide, cells), jnp.bfloat16)
    response = pl.pallas_call(
        functools.partial(respond_kernel, count, grids, kinds),
        out_shape=pltpu.VMEM((PAIR, half, rows, cells), f32),
        in_specs=[hbm] * 6,
        out_specs=vmem,
        scratch_shapes=[
            pltpu.SMEM(owner.shape, owner.dtype),
            pltpu.SMEM(shifts.shape, shifts.dtype),
            pltpu.SMEM(occupation.shape, occupation.dtype),
            pltpu.VMEM((half, rows, cells), f32),
            slots, slots, slots, slots,
            pltpu.VMEM((half, planes, cells), f32),
            pltpu.VMEM((PAIR * orbital_count, planes, cells), f32),
            pltpu.VMEM((planes, cells), f32),
            pltpu.VMEM((PAIR, 2 * orbital_count, LANES), f32),
            pltpu.VMEM((half, rows, cells), f32),
            pltpu.VMEM((cells // LANES, rows * wide, LANES), f32),
            slots, slots, slots, slots, slots, slots, slots, slots,
            big, big, big, pltpu.VMEM((rows, wide, cells), f32), big, big,
            packed, packed, packed, packed,
            pltpu.VMEM((planes * wide, WIDTH), f32),
            pltpu.VMEM((2 * WIDTH, WIDTH), jnp.bfloat16),
            dma((3,)), dma((2 + orbital_count,)), dma((2, chunks)), dma((4, chunks)), dma((4, chunks)),
            dma((2, 2, half)), dma((2, 2, 1 + 2 * orbital_count)), dma((2, 1 + orbital_count)),
            dma((2, chunks)),
        ],
        compiler_params=pltpu.CompilerParams(collective_id=0, has_side_effects=True),
        name="respond",
    )(owner, shifts, occupation, stored, orbitals, local_pot)
    return response.reshape(1, blocks, kinds, rows, cells)


def solution(mesh):
    in_specs = (
        P("orb", None, None, "grid", None),
        P("orb", "grid", None),
        P("grid", None),
        P("orb"),
        P("orb"),
        P(),
    )
    out_specs = P("orb", None, None, "grid", None)
    body = functools.partial(shards, mesh.shape["orb"], mesh.shape["grid"])
    return jax.shard_map(body, mesh=mesh, in_specs=in_specs, out_specs=out_specs, check_vma=False)
```

```python
import functools

import jax
import jax.numpy as jnp
from jax import lax
from jax.experimental import pallas as pl
from jax.experimental.pallas import tpu as pltpu
from jax.sharding import PartitionSpec as P

NZ = 32
ITERS = 4
REACH = 2
HALO = REACH * ITERS
KINETIC_DIAG = 3.75
PAIR = 2
MESH = pl.DeviceIdType.MESH


class Ring:
    def __init__(self, count, grids):
        self.count, self.lines, self.grids = count, count // PAIR, grids
        self.me = lax.axis_index("orb")
        self.row = lax.axis_index("grid")
        self.line, self.side = self.me // PAIR, self.me % PAIR
        self.partner = self.line * PAIR + (1 - self.side)

    def at_line(self, line):
        return {"orb": line * PAIR + self.side, "grid": self.row}

    def across(self):
        return {"orb": self.partner, "grid": self.row}

    def up(self):
        return {"orb": self.me, "grid": self.row - 1}

    def down(self):
        return {"orb": self.me, "grid": self.row + 1}


def greet_peers(ring):
    barrier = pltpu.get_barrier_semaphore()
    top = ring.lines - 1

    def greet(target):
        pl.semaphore_signal(barrier, inc=1, device_id=target, device_id_type=MESH)

    greet(ring.across())

    @pl.when(ring.line > 0)
    def _():
        greet(ring.at_line(ring.line - 1))

    @pl.when(ring.line < top)
    def _():
        greet(ring.at_line(ring.line + 1))

    peers = 1 + (ring.line + top) // ring.lines + (2 * top - ring.line) // ring.lines
    @pl.when(ring.row > 0)
    def _():
        greet(ring.up())

    @pl.when(ring.row < ring.grids - 1)
    def _():
        greet(ring.down())

    last = ring.grids - 1
    peers = peers + (ring.row + last) // ring.grids + (2 * last - ring.row) // ring.grids
    return barrier, peers


def send(src, dst, send_sem, recv_sem, target):
    return pltpu.make_async_remote_copy(
        src_ref=src, dst_ref=dst, send_sem=send_sem, recv_sem=recv_sem,
        device_id=target, device_id_type=MESH,
    )


SPLIT = 1
SPREAD_LAG = 4
FORWARD = 8
FORWARD_STEP = 2
GATHER_LAG = 4
LANES = 128
WIDTH = 256


class Waves:
    def __init__(self, ring, chunks, lag, buffers, sems):
        self.ring, self.chunks, self.lag, self.sems = ring, chunks, lag, sems
        self.from_left, self.from_right, self.to_right, self.to_left = buffers
        self.has_left, self.has_right = ring.line > 0, ring.line < ring.lines - 1

    def right(self, q, target):
        sems = self.sems
        return send(self.to_right.at[q], self.from_left.at[q], sems.at[0, q], sems.at[1, q], target)

    def left(self, q, target):
        sems = self.sems
        return send(self.to_left.at[q], self.from_right.at[q], sems.at[2, q], sems.at[3, q], target)

    def clear(self):
        @pl.when(jnp.logical_not(self.has_left))
        def _():
            self.from_left[...] = jnp.zeros_like(self.from_left)

        @pl.when(jnp.logical_not(self.has_right))
        def _():
            self.from_right[...] = jnp.zeros_like(self.from_right)

    def begin(self, q, value):
        @pl.when(jnp.logical_not(self.has_left) & self.has_right)
        def _():
            self.to_right[q] = value
            self.right(q, self.ring.at_line(self.ring.line + 1)).start()

        @pl.when(jnp.logical_not(self.has_right) & self.has_left)
        def _():
            self.to_left[q] = value
            self.left(q, self.ring.at_line(self.ring.line - 1)).start()

    def run(self, low, high, prepare, onward, finish):
        ring, lag, line, top = self.ring, self.lag, self.ring.line, self.ring.lines - 1
        beyond = (2 * line) // ring.lines
        late = beyond * line + (1 - beyond) * (top - line)

        def step(s, carry):
            def event(offset, act):
                q = s - offset

                @pl.when((q >= 0) & (q < self.chunks))
                def _():
                    act(q)

            def rightward(q):
                @pl.when(self.has_left)
                def _():
                    self.right(q, ring.across()).wait_recv()

                @pl.when(self.has_left & self.has_right)
                def _():
                    self.to_right[q] = onward(q, self.from_left[q])
                    self.right(q, ring.at_line(line + 1)).start()

            def leftward(q):
                @pl.when(self.has_right)
                def _():
                    self.left(q, ring.across()).wait_recv()

                @pl.when(self.has_left & self.has_right)
                def _():
                    self.to_left[q] = onward(q, self.from_right[q])
                    self.left(q, ring.at_line(line - 1)).start()

            event(0, prepare)
            event(line * lag, rightward)
            event((top - line) * lag, leftward)
            event(late * lag, finish)
            return carry

        lax.fori_loop(low, high, step, 0)

    def steps(self):
        return self.chunks + (self.ring.lines - 1) * self.lag

    def drain(self):
        @pl.when(self.has_right)
        def _():
            for q in range(self.chunks):
                self.right(q, self.ring.across()).wait_send()

        @pl.when(self.has_left)
        def _():
            for q in range(self.chunks):
                self.left(q, self.ring.across()).wait_send()


def chunk_of(ref, q, per, start=0):
    width = ref.shape[-1] // SPLIT
    piece = q % per
    rows = pl.ds(pl.multiple_of(start + piece // SPLIT * HALO, HALO), HALO)
    return ref.at[q // per, rows, pl.ds(pl.multiple_of(piece % SPLIT * width, LANES), width)]


def band_matrix(depth, width):
    k = lax.broadcasted_iota(jnp.int32, (depth, width), 0)
    n = lax.broadcasted_iota(jnp.int32, (depth, width), 1) + width // 2
    far_y, far_z = jnp.abs(k // NZ - n // NZ), jnp.abs(k % NZ - n % NZ)
    near = ((far_y == 1) & (far_z == 0)) | ((far_y == 0) & (far_z == 1))
    far = ((far_y == 2) & (far_z == 0)) | ((far_y == 0) & (far_z == 2))
    return jnp.where(near, 16.0, jnp.where(far, -1.0, 0.0)).astype(jnp.bfloat16)


def split(value):
    high = value.astype(jnp.bfloat16)
    return high, (value - high.astype(jnp.float32)).astype(jnp.bfloat16)


class Sweeps:
    def __init__(self, trial, orbs, local, pack, density, scratch):
        self.inverse = scratch[5]
        self.trial, self.orbs, self.local, self.pack, self.density = trial, orbs, local, pack, density
        (
            self.first, self.scale, self.source, self.weighted, self.now_a, self.now_b,
            self.hi_a, self.hi_b, self.lo_a, self.lo_b, self.product, self.band,
        ) = scratch
        self.batch = orbs.shape[0]
        self.planes, self.cells = local.shape

    def start(self):
        self.band[...] = band_matrix(2 * WIDTH, WIDTH)

    def column(self, kind):
        size = self.batch // PAIR
        ours, theirs = self.pack[0, kind * size : (kind + 1) * size], self.pack[1, kind * size : (kind + 1) * size]
        return jnp.broadcast_to(jnp.concatenate([ours, theirs], axis=0)[:, 0:1], (self.batch, self.cells))

    def divide(self, planes, inside):
        shift = self.column(0)
        for p in planes:
            here = jnp.broadcast_to(self.local[p : p + 1, :], (self.batch, self.cells))
            inverse = 1.0 / (KINETIC_DIAG + (here + shift))
            if inside is not None:
                inverse = jnp.where(inside, inverse, 0.0)
            self.inverse[p] = inverse
            self.scale[p] = inverse * (1.0 / 24.0)

    def combine(self, planes, center):
        batch, cells = self.batch, self.cells
        which = lax.broadcasted_iota(jnp.int32, (batch, cells), 0)
        weight = self.column(1) if center else None
        for p in planes:
            orb = jnp.broadcast_to(self.orbs[0, p : p + 1, :], (batch, cells))
            for n in range(1, batch):
                other = jnp.broadcast_to(self.orbs[n, p : p + 1, :], (batch, cells))
                orb = jnp.where(which < n, orb, other)
            self.source[p] = -(orb * self.inverse[p])
            if center:
                self.weighted[p - HALO] = weight * orb

    def run(self, t):
        planes, cells, first, scale = self.planes, self.cells, self.first, self.scale
        batch = self.batch
        for x in range(0, planes, 2):
            values = []
            for p in (x, x + 1):
                value = jnp.broadcast_to(self.trial[t, p : p + 1, :], (batch, cells)) * self.source[p]
                first[p] = value
                values.append(value)
            high, low = split(jnp.concatenate(values, axis=0))
            self.hi_a[x * batch : (x + 2) * batch] = high
            self.lo_a[x * batch : (x + 2) * batch] = low
        current = first
        buffers = ((self.now_a, self.hi_a, self.lo_a), (self.now_b, self.hi_b, self.lo_b))
        product = self.product
        for repeat in range(ITERS):
            hi_in, lo_in = buffers[repeat % 2][1:]
            target, hi_out, lo_out = buffers[(repeat + 1) % 2]
            margin = REACH * (repeat + 1)
            extent = planes - 2 * margin
            for left in range(0, cells, WIDTH):
                a = max(0, left - WIDTH // 2)
                b = min(cells, left + WIDTH + WIDTH // 2)
                k = a - (left - WIDTH // 2)
                weights = self.band[k : k + b - a, :]
                span = slice(margin * batch, (margin + extent) * batch)
                product[0 : extent * batch] = jnp.dot(
                    hi_in[span, a:b], weights, preferred_element_type=jnp.float32
                ) + jnp.dot(lo_in[span, a:b], weights, preferred_element_type=jnp.float32)
                lanes = slice(left, left + WIDTH)
                for x in range(margin, margin + extent, 2):
                    values = []
                    for p in (x, x + 1):
                        near = current[p - 1, :, lanes] + current[p + 1, :, lanes]
                        far = current[p - 2, :, lanes] + current[p + 2, :, lanes]
                        spot = (p - margin) * batch
                        moved = product[spot : spot + batch] + (16.0 * near - far)
                        value = first[p, :, lanes] + scale[p, :, lanes] * moved
                        if repeat == ITERS - 1:
                            where = slice((p - margin) * batch, (p - margin + 1) * batch)
                            term = self.weighted[p - margin, :, lanes] * value
                            for c in range(WIDTH // LANES):
                                block = left // LANES + c
                                self.density[block, where, :] = term[:, c * LANES : (c + 1) * LANES]
                        else:
                            target[p, :, lanes] = value
                            values.append(value)
                    if values:
                        high, low = split(jnp.concatenate(values, axis=0))
                        hi_out[x * batch : (x + 2) * batch, lanes] = high
                        lo_out[x * batch : (x + 2) * batch, lanes] = low
            current = target

    def collect(self, c):
        base = c * HALO * self.batch
        pieces = []
        for block in range(self.cells // LANES):
            total = self.density[block, pl.ds(base, HALO, stride=self.batch), :]
            for n in range(1, self.batch):
                total = total + self.density[block, pl.ds(base + n, HALO, stride=self.batch), :]
            pieces.append(total)
        return jnp.concatenate(pieces, axis=1)


def respond_kernel(
    count, grids, kinds, owner_hbm, shift_hbm, weight_hbm, pot_ref, orb_ref, local_ref, out_ref,
    owner_ref, shift_ref, weight_ref, mine, crossed, merged, ours, theirs_total, trial, orbs, local, pack, part, density,
    s_left, s_right, s_rightward, s_leftward, r_left, r_right, r_rightward, r_leftward,
    first, scale, source, weighted, now_a, now_b, hi_a, hi_b, lo_a, lo_b, product, band,
    scalar_sems, load_sems, cross_sems, s_sems, r_sems, halo_sems, edge_sems, pair_sems, side_sems,
):
    ring = Ring(count, grids)
    orbitals, rows, cells = orb_ref.shape
    half = pot_ref.shape[1]
    per = rows // HALO * SPLIT
    chunks = half * per
    last = HALO + rows
    has_up, has_down = ring.row > 0, ring.row < grids - 1
    spread = Waves(ring, chunks, SPREAD_LAG, (s_left, s_right, s_rightward, s_leftward), s_sems)
    gather = Waves(ring, chunks, GATHER_LAG, (r_left, r_right, r_rightward, r_leftward), r_sems)
    sweeps = Sweeps(
        trial, orbs, local, pack, density,
        (first, scale, source, weighted, now_a, now_b, hi_a, hi_b, lo_a, lo_b, product, band),
    )

    def orb_rows(k, n, start, size):
        return orbs.at[k * orbitals + n, pl.ds(start, size)]

    barrier, peers = greet_peers(ring)
    loads = [
        pltpu.make_async_copy(pot_ref.at[ring.side], mine, load_sems.at[0]),
        pltpu.make_async_copy(local_ref, local.at[pl.ds(HALO, rows)], load_sems.at[1]),
    ] + [
        pltpu.make_async_copy(orb_ref.at[n], orb_rows(0, n, HALO, rows), load_sems.at[2 + n])
        for n in range(orbitals)
    ]
    scalars = [
        pltpu.make_async_copy(src, dst, scalar_sems.at[i])
        for i, (src, dst) in enumerate(
            [(shift_hbm, shift_ref), (weight_hbm, weight_ref), (owner_hbm, owner_ref)]
        )
    ]
    for load in scalars + loads:
        load.start()
    pl.semaphore_wait(barrier, peers)

    def cross(q):
        return send(
            chunk_of(pot_ref.at[1 - ring.side], q, per), crossed.at[q],
            cross_sems.at[0, q], cross_sems.at[1, q], ring.across(),
        )

    for q in range(per):
        cross(q).start()

    def center(n):
        return send(
            orb_ref.at[n], orb_rows(1, n, HALO, rows),
            pair_sems.at[0, n], pair_sems.at[1, n], ring.across(),
        )

    def edge_up(k, target):
        if k == 0:
            src, dst = local_ref.at[pl.ds(0, HALO)], local.at[pl.ds(last, HALO)]
        elif k <= orbitals:
            src, dst = orb_ref.at[k - 1, pl.ds(0, HALO)], orb_rows(0, k - 1, last, HALO)
        else:
            n = k - 1 - orbitals
            src, dst = orb_rows(1, n, HALO, HALO), orb_rows(1, n, last, HALO)
        return send(src, dst, edge_sems.at[0, 0, k], edge_sems.at[1, 0, k], target)

    def edge_down(k, target):
        if k == 0:
            src, dst = local_ref.at[pl.ds(rows - HALO, HALO)], local.at[pl.ds(0, HALO)]
        elif k <= orbitals:
            src, dst = orb_ref.at[k - 1, pl.ds(rows - HALO, HALO)], orb_rows(0, k - 1, 0, HALO)
        else:
            n = k - 1 - orbitals
            src, dst = orb_rows(1, n, rows, HALO), orb_rows(1, n, 0, HALO)
        return send(src, dst, edge_sems.at[0, 1, k], edge_sems.at[1, 1, k], target)

    own = range(0, 1 + orbitals)
    theirs = range(1 + orbitals, 1 + 2 * orbitals)

    def start_edges(which):
        @pl.when(has_up)
        def _():
            for k in which:
                edge_up(k, ring.up()).start()

        @pl.when(has_down)
        def _():
            for k in which:
                edge_down(k, ring.down()).start()

    def await_edges(which):
        @pl.when(has_up)
        def _():
            for k in which:
                edge_down(k, ring.across()).wait_recv()

        @pl.when(has_down)
        def _():
            for k in which:
                edge_up(k, ring.across()).wait_recv()

    for load in scalars:
        load.wait()
    for n in range(orbitals):
        pack[0, n] = jnp.full((LANES,), shift_ref[n], jnp.float32)
        pack[0, orbitals + n] = jnp.full((LANES,), weight_ref[n].astype(jnp.float32), jnp.float32)
    start_edges(own)
    share = send(pack.at[0], pack.at[1], pair_sems.at[0, orbitals], pair_sems.at[1, orbitals], ring.across())
    share.start()
    for q in range(per, chunks):
        cross(q).start()
    for n in range(orbitals):
        center(n).start()
    gather.clear()

    def clear(start):
        orbs[:, start : start + HALO] = jnp.zeros((PAIR * orbitals, HALO, cells), jnp.float32)
        local[start : start + HALO] = jnp.zeros((HALO, cells), jnp.float32)
        trial[:, start : start + HALO] = jnp.zeros((half, HALO, cells), jnp.float32)

    @pl.when(jnp.logical_not(has_up))
    def _():
        clear(0)

    @pl.when(jnp.logical_not(has_down))
    def _():
        clear(last)

    sweeps.start()
    loads[0].wait()

    def owner_of(q):
        return owner_ref[(ring.side * half + q // per) // kinds]

    def halo_up(t, target):
        return send(
            trial.at[t, pl.ds(HALO, HALO)], trial.at[t, pl.ds(last, HALO)],
            halo_sems.at[0, 0, t], halo_sems.at[1, 0, t], target,
        )

    def halo_down(t, target):
        return send(
            trial.at[t, pl.ds(rows, HALO)], trial.at[t, pl.ds(0, HALO)],
            halo_sems.at[0, 1, t], halo_sems.at[1, 1, t], target,
        )

    def merge(q):
        cross(q).wait_recv()
        value = jnp.where(owner_of(q) == ring.partner, crossed[q], chunk_of(mine, q, per)[...])
        merged[q] = value
        spread.begin(q, jnp.where(owner_of(q) // PAIR == ring.line, value, 0.0))

    def select(q, came):
        return jnp.where(owner_of(q) // PAIR == ring.line, merged[q], came)

    def settle(q):
        place = owner_of(q) // PAIR
        other = jnp.where(place < ring.line, s_left[q], s_right[q])
        chunk_of(trial, q, per, HALO)[...] = jnp.where(place == ring.line, merged[q], other)

        @pl.when(has_up & (q % per == SPLIT - 1))
        def _():
            halo_up(q // per, ring.up()).start()

        @pl.when(has_down & (q % per == per - 1))
        def _():
            halo_down(q // per, ring.down()).start()

    inner, outer = range(HALO, last), (range(0, HALO), range(last, last + HALO))
    spread.run(0, SPREAD_LAG, merge, select, settle)
    share.wait_recv()
    loads[1].wait()
    sweeps.divide(inner, None)
    spread.run(SPREAD_LAG, FORWARD, merge, select, settle)
    for n in range(orbitals):
        center(n).wait_recv()
        start_edges([theirs[n]])
        spread.run(FORWARD + FORWARD_STEP * n, FORWARD + FORWARD_STEP * (n + 1), merge, select, settle)
    first_trial = FORWARD + FORWARD_STEP * orbitals
    for load in loads[2:]:
        load.wait()
    sweeps.combine(inner, True)
    await_edges(own)
    sweeps.divide(outer[0], has_up)
    sweeps.divide(outer[1], has_down)
    begin = max((ring.lines - 1) * SPREAD_LAG + per, first_trial)
    spread.run(first_trial, begin, merge, select, settle)
    await_edges(theirs)
    sweeps.combine(outer[0], False)
    sweeps.combine(outer[1], False)

    def add(q, came):
        return came + chunk_of(part, q, per)[...]

    def across(q):
        return send(
            ours.at[q], theirs_total.at[q], side_sems.at[0, q], side_sems.at[1, q], ring.across()
        )

    def keep(side, q, value):
        owned = owner_ref[(side * half + q // per) // kinds] == ring.me
        chunk_of(out_ref.at[side], q, per)[...] = jnp.where(owned, value, 0.0)

    def finish(q):
        total = r_left[q] + chunk_of(part, q, per)[...] + r_right[q]
        ours[q] = total
        across(q).start()
        keep(ring.side, q, total)

    def item(t, carry):
        @pl.when(has_up)
        def _():
            halo_down(t, ring.across()).wait_recv()

        @pl.when(has_down)
        def _():
            halo_up(t, ring.across()).wait_recv()

        sweeps.run(t)

        @pl.when(t == 0)
        def _():
            spread.run(begin, spread.steps(), merge, select, settle)

        for c in range(per // SPLIT):
            value = sweeps.collect(c)
            part[t, c * HALO : (c + 1) * HALO] = value
            width = cells // SPLIT
            for j in range(SPLIT):
                gather.begin(t * per + c * SPLIT + j, value[:, j * width : (j + 1) * width])
        gather.run((t - 1) * per + 1, t * per + 1, lambda q: None, add, finish)
        return carry

    lax.fori_loop(0, half, item, 0)
    gather.run((half - 1) * per + 1, gather.steps(), lambda q: None, add, finish)

    def sent(which):
        @pl.when(has_up)
        def _():
            for k in which:
                edge_up(k, ring.across()).wait_send()

        @pl.when(has_down)
        def _():
            for k in which:
                edge_down(k, ring.across()).wait_send()

    sent(own)
    sent(theirs)

    @pl.when(has_up)
    def _():
        for t in range(half):
            halo_up(t, ring.across()).wait_send()

    @pl.when(has_down)
    def _():
        for t in range(half):
            halo_down(t, ring.across()).wait_send()

    share.wait_send()
    for n in range(orbitals):
        center(n).wait_send()
    for q in range(chunks):
        cross(q).wait_send()
    spread.drain()
    gather.drain()
    for q in range(chunks):
        across(q).wait_recv()
        keep(1 - ring.side, q, theirs_total[q])
        across(q).wait_send()


def shards(count, grids, potentials, orbitals, local_pot, shifts, occupation, owner):
    _, blocks, kinds, rows, cells = potentials.shape
    batch = blocks * kinds
    half = batch // PAIR
    orbital_count = orbitals.shape[0]
    planes = rows + 2 * HALO
    wide = PAIR * orbital_count
    stored = potentials.reshape(PAIR, half, rows, cells)
    vmem = pl.BlockSpec(memory_space=pltpu.VMEM)
    hbm = pl.BlockSpec(memory_space=pl.ANY)
    f32 = jnp.float32
    dma = pltpu.SemaphoreType.DMA
    chunks = half * (rows // HALO) * SPLIT
    slots = pltpu.VMEM((chunks, HALO, cells // SPLIT), f32)
    big = pltpu.VMEM((planes, wide, cells), f32)
    packed = pltpu.VMEM((planes * wide, cells), jnp.bfloat16)
    response = pl.pallas_call(
        functools.partial(respond_kernel, count, grids, kinds),
        out_shape=pltpu.VMEM((PAIR, half, rows, cells), f32),
        in_specs=[hbm] * 6,
        out_specs=vmem,
        scratch_shapes=[
            pltpu.SMEM(owner.shape, owner.dtype),
            pltpu.SMEM(shifts.shape, shifts.dtype),
            pltpu.SMEM(occupation.shape, occupation.dtype),
            pltpu.VMEM((half, rows, cells), f32),
            slots, slots, slots, slots,
            pltpu.VMEM((half, planes, cells), f32),
            pltpu.VMEM((PAIR * orbital_count, planes, cells), f32),
            pltpu.VMEM((planes, cells), f32),
            pltpu.VMEM((PAIR, 2 * orbital_count, LANES), f32),
            pltpu.VMEM((half, rows, cells), f32),
            pltpu.VMEM((cells // LANES, rows * wide, LANES), f32),
            slots, slots, slots, slots, slots, slots, slots, slots,
            big, big, big, pltpu.VMEM((rows, wide, cells), f32), big, big,
            packed, packed, packed, packed,
            pltpu.VMEM((planes * wide, WIDTH), f32),
            pltpu.VMEM((2 * WIDTH, WIDTH), jnp.bfloat16),
            dma((3,)), dma((2 + orbital_count,)), dma((2, chunks)), dma((4, chunks)), dma((4, chunks)),
            dma((2, 2, half)), dma((2, 2, 1 + 2 * orbital_count)), dma((2, 1 + orbital_count)),
            dma((2, chunks)),
        ],
        compiler_params=pltpu.CompilerParams(collective_id=0, has_side_effects=True),
        name="respond",
    )(owner, shifts, occupation, stored, orbitals, local_pot)
    return response.reshape(1, blocks, kinds, rows, cells)


def solution(mesh):
    in_specs = (
        P("orb", None, None, "grid", None),
        P("orb", "grid", None),
        P("grid", None),
        P("orb"),
        P("orb"),
        P(),
    )
    out_specs = P("orb", None, None, "grid", None)
    body = functools.partial(shards, mesh.shape["orb"], mesh.shape["grid"])
    return jax.shard_map(body, mesh=mesh, in_specs=in_specs, out_specs=out_specs, check_vma=False)
```

```python
import functools

import jax
import jax.numpy as jnp
from jax import lax
from jax.experimental import pallas as pl
from jax.experimental.pallas import tpu as pltpu
from jax.sharding import PartitionSpec as P

NZ = 32
ITERS = 4
REACH = 2
HALO = REACH * ITERS
KINETIC_DIAG = 3.75
PAIR = 2
MESH = pl.DeviceIdType.MESH


class Ring:
    def __init__(self, count, grids):
        self.count, self.lines, self.grids = count, count // PAIR, grids
        self.me = lax.axis_index("orb")
        self.row = lax.axis_index("grid")
        self.line, self.side = self.me // PAIR, self.me % PAIR
        self.partner = self.line * PAIR + (1 - self.side)

    def at_line(self, line):
        return {"orb": line * PAIR + self.side, "grid": self.row}

    def across(self):
        return {"orb": self.partner, "grid": self.row}

    def up(self):
        return {"orb": self.me, "grid": self.row - 1}

    def down(self):
        return {"orb": self.me, "grid": self.row + 1}


def greet_peers(ring):
    barrier = pltpu.get_barrier_semaphore()
    top = ring.lines - 1

    def greet(target):
        pl.semaphore_signal(barrier, inc=1, device_id=target, device_id_type=MESH)

    greet(ring.across())

    @pl.when(ring.line > 0)
    def _():
        greet(ring.at_line(ring.line - 1))

    @pl.when(ring.line < top)
    def _():
        greet(ring.at_line(ring.line + 1))

    peers = 1 + (ring.line + top) // ring.lines + (2 * top - ring.line) // ring.lines
    @pl.when(ring.row > 0)
    def _():
        greet(ring.up())

    @pl.when(ring.row < ring.grids - 1)
    def _():
        greet(ring.down())

    last = ring.grids - 1
    peers = peers + (ring.row + last) // ring.grids + (2 * last - ring.row) // ring.grids
    return barrier, peers


def send(src, dst, send_sem, recv_sem, target):
    return pltpu.make_async_remote_copy(
        src_ref=src, dst_ref=dst, send_sem=send_sem, recv_sem=recv_sem,
        device_id=target, device_id_type=MESH,
    )


SPLIT = 1
SPREAD_LAG = 5
FORWARD = 8
FORWARD_STEP = 2
GATHER_LAG = 4
LANES = 128
WIDTH = 256


class Waves:
    def __init__(self, ring, chunks, lag, buffers, sems):
        self.ring, self.chunks, self.lag, self.sems = ring, chunks, lag, sems
        self.from_left, self.from_right, self.to_right, self.to_left = buffers
        self.has_left, self.has_right = ring.line > 0, ring.line < ring.lines - 1

    def right(self, q, target):
        sems = self.sems
        return send(self.to_right.at[q], self.from_left.at[q], sems.at[0, q], sems.at[1, q], target)

    def left(self, q, target):
        sems = self.sems
        return send(self.to_left.at[q], self.from_right.at[q], sems.at[2, q], sems.at[3, q], target)

    def clear(self):
        @pl.when(jnp.logical_not(self.has_left))
        def _():
            self.from_left[...] = jnp.zeros_like(self.from_left)

        @pl.when(jnp.logical_not(self.has_right))
        def _():
            self.from_right[...] = jnp.zeros_like(self.from_right)

    def begin(self, q, value):
        @pl.when(jnp.logical_not(self.has_left) & self.has_right)
        def _():
            self.to_right[q] = value
            self.right(q, self.ring.at_line(self.ring.line + 1)).start()

        @pl.when(jnp.logical_not(self.has_right) & self.has_left)
        def _():
            self.to_left[q] = value
            self.left(q, self.ring.at_line(self.ring.line - 1)).start()

    def run(self, low, high, prepare, onward, finish):
        ring, lag, line, top = self.ring, self.lag, self.ring.line, self.ring.lines - 1
        beyond = (2 * line) // ring.lines
        late = beyond * line + (1 - beyond) * (top - line)

        def step(s, carry):
            def event(offset, act):
                q = s - offset

                @pl.when((q >= 0) & (q < self.chunks))
                def _():
                    act(q)

            def rightward(q):
                @pl.when(self.has_left)
                def _():
                    self.right(q, ring.across()).wait_recv()

                @pl.when(self.has_left & self.has_right)
                def _():
                    self.to_right[q] = onward(q, self.from_left[q])
                    self.right(q, ring.at_line(line + 1)).start()

            def leftward(q):
                @pl.when(self.has_right)
                def _():
                    self.left(q, ring.across()).wait_recv()

                @pl.when(self.has_left & self.has_right)
                def _():
                    self.to_left[q] = onward(q, self.from_right[q])
                    self.left(q, ring.at_line(line - 1)).start()

            event(0, prepare)
            event(line * lag, rightward)
            event((top - line) * lag, leftward)
            event(late * lag, finish)
            return carry

        lax.fori_loop(low, high, step, 0)

    def steps(self):
        return self.chunks + (self.ring.lines - 1) * self.lag

    def drain(self):
        @pl.when(self.has_right)
        def _():
            for q in range(self.chunks):
                self.right(q, self.ring.across()).wait_send()

        @pl.when(self.has_left)
        def _():
            for q in range(self.chunks):
                self.left(q, self.ring.across()).wait_send()


def chunk_of(ref, q, per, start=0):
    width = ref.shape[-1] // SPLIT
    piece = q % per
    rows = pl.ds(pl.multiple_of(start + piece // SPLIT * HALO, HALO), HALO)
    return ref.at[q // per, rows, pl.ds(pl.multiple_of(piece % SPLIT * width, LANES), width)]


def band_matrix(depth, width):
    k = lax.broadcasted_iota(jnp.int32, (depth, width), 0)
    n = lax.broadcasted_iota(jnp.int32, (depth, width), 1) + width // 2
    far_y, far_z = jnp.abs(k // NZ - n // NZ), jnp.abs(k % NZ - n % NZ)
    near = ((far_y == 1) & (far_z == 0)) | ((far_y == 0) & (far_z == 1))
    far = ((far_y == 2) & (far_z == 0)) | ((far_y == 0) & (far_z == 2))
    return jnp.where(near, 16.0, jnp.where(far, -1.0, 0.0)).astype(jnp.bfloat16)


def split(value):
    high = value.astype(jnp.bfloat16)
    return high, (value - high.astype(jnp.float32)).astype(jnp.bfloat16)


class Sweeps:
    def __init__(self, trial, orbs, local, pack, density, scratch):
        self.inverse = scratch[5]
        self.trial, self.orbs, self.local, self.pack, self.density = trial, orbs, local, pack, density
        (
            self.first, self.scale, self.source, self.weighted, self.now_a, self.now_b,
            self.hi_a, self.hi_b, self.lo_a, self.lo_b, self.product, self.band,
        ) = scratch
        self.batch = orbs.shape[0]
        self.planes, self.cells = local.shape

    def start(self):
        self.band[...] = band_matrix(2 * WIDTH, WIDTH)

    def column(self, kind):
        size = self.batch // PAIR
        ours, theirs = self.pack[0, kind * size : (kind + 1) * size], self.pack[1, kind * size : (kind + 1) * size]
        return jnp.broadcast_to(jnp.concatenate([ours, theirs], axis=0)[:, 0:1], (self.batch, self.cells))

    def divide(self, planes, inside):
        shift = self.column(0)
        for p in planes:
            here = jnp.broadcast_to(self.local[p : p + 1, :], (self.batch, self.cells))
            inverse = 1.0 / (KINETIC_DIAG + (here + shift))
            if inside is not None:
                inverse = jnp.where(inside, inverse, 0.0)
            self.inverse[p] = inverse
            self.scale[p] = inverse * (1.0 / 24.0)

    def combine(self, planes, center):
        batch, cells = self.batch, self.cells
        which = lax.broadcasted_iota(jnp.int32, (batch, cells), 0)
        weight = self.column(1) if center else None
        for p in planes:
            orb = jnp.broadcast_to(self.orbs[0, p : p + 1, :], (batch, cells))
            for n in range(1, batch):
                other = jnp.broadcast_to(self.orbs[n, p : p + 1, :], (batch, cells))
                orb = jnp.where(which < n, orb, other)
            self.source[p] = -(orb * self.inverse[p])
            if center:
                self.weighted[p - HALO] = weight * orb

    def run(self, t):
        planes, cells, first, scale = self.planes, self.cells, self.first, self.scale
        batch = self.batch
        for x in range(0, planes, 2):
            values = []
            for p in (x, x + 1):
                value = jnp.broadcast_to(self.trial[t, p : p + 1, :], (batch, cells)) * self.source[p]
                first[p] = value
                values.append(value)
            high, low = split(jnp.concatenate(values, axis=0))
            self.hi_a[x * batch : (x + 2) * batch] = high
            self.lo_a[x * batch : (x + 2) * batch] = low
        current = first
        buffers = ((self.now_a, self.hi_a, self.lo_a), (self.now_b, self.hi_b, self.lo_b))
        product = self.product
        for repeat in range(ITERS):
            hi_in, lo_in = buffers[repeat % 2][1:]
            target, hi_out, lo_out = buffers[(repeat + 1) % 2]
            margin = REACH * (repeat + 1)
            extent = planes - 2 * margin
            for left in range(0, cells, WIDTH):
                a = max(0, left - WIDTH // 2)
                b = min(cells, left + WIDTH + WIDTH // 2)
                k = a - (left - WIDTH // 2)
                weights = self.band[k : k + b - a, :]
                span = slice(margin * batch, (margin + extent) * batch)
                product[0 : extent * batch] = jnp.dot(
                    hi_in[span, a:b], weights, preferred_element_type=jnp.float32
                ) + jnp.dot(lo_in[span, a:b], weights, preferred_element_type=jnp.float32)
                lanes = slice(left, left + WIDTH)
                for x in range(margin, margin + extent, 2):
                    values = []
                    for p in (x, x + 1):
                        near = current[p - 1, :, lanes] + current[p + 1, :, lanes]
                        far = current[p - 2, :, lanes] + current[p + 2, :, lanes]
                        spot = (p - margin) * batch
                        moved = product[spot : spot + batch] + (16.0 * near - far)
                        value = first[p, :, lanes] + scale[p, :, lanes] * moved
                        if repeat == ITERS - 1:
                            where = slice((p - margin) * batch, (p - margin + 1) * batch)
                            term = self.weighted[p - margin, :, lanes] * value
                            for c in range(WIDTH // LANES):
                                block = left // LANES + c
                                self.density[block, where, :] = term[:, c * LANES : (c + 1) * LANES]
                        else:
                            target[p, :, lanes] = value
                            values.append(value)
                    if values:
                        high, low = split(jnp.concatenate(values, axis=0))
                        hi_out[x * batch : (x + 2) * batch, lanes] = high
                        lo_out[x * batch : (x + 2) * batch, lanes] = low
            current = target

    def collect(self, c):
        base = c * HALO * self.batch
        pieces = []
        for block in range(self.cells // LANES):
            total = self.density[block, pl.ds(base, HALO, stride=self.batch), :]
            for n in range(1, self.batch):
                total = total + self.density[block, pl.ds(base + n, HALO, stride=self.batch), :]
            pieces.append(total)
        return jnp.concatenate(pieces, axis=1)


def respond_kernel(
    count, grids, kinds, owner_hbm, shift_hbm, weight_hbm, pot_ref, orb_ref, local_ref, out_ref,
    owner_ref, shift_ref, weight_ref, mine, crossed, merged, ours, theirs_total, trial, orbs, local, pack, part, density,
    s_left, s_right, s_rightward, s_leftward, r_left, r_right, r_rightward, r_leftward,
    first, scale, source, weighted, now_a, now_b, hi_a, hi_b, lo_a, lo_b, product, band,
    scalar_sems, load_sems, cross_sems, s_sems, r_sems, halo_sems, edge_sems, pair_sems, side_sems,
):
    ring = Ring(count, grids)
    orbitals, rows, cells = orb_ref.shape
    half = pot_ref.shape[1]
    per = rows // HALO * SPLIT
    chunks = half * per
    last = HALO + rows
    has_up, has_down = ring.row > 0, ring.row < grids - 1
    spread = Waves(ring, chunks, SPREAD_LAG, (s_left, s_right, s_rightward, s_leftward), s_sems)
    gather = Waves(ring, chunks, GATHER_LAG, (r_left, r_right, r_rightward, r_leftward), r_sems)
    sweeps = Sweeps(
        trial, orbs, local, pack, density,
        (first, scale, source, weighted, now_a, now_b, hi_a, hi_b, lo_a, lo_b, product, band),
    )

    def orb_rows(k, n, start, size):
        return orbs.at[k * orbitals + n, pl.ds(start, size)]

    barrier, peers = greet_peers(ring)
    loads = [
        pltpu.make_async_copy(pot_ref.at[ring.side], mine, load_sems.at[0]),
        pltpu.make_async_copy(local_ref, local.at[pl.ds(HALO, rows)], load_sems.at[1]),
    ] + [
        pltpu.make_async_copy(orb_ref.at[n], orb_rows(0, n, HALO, rows), load_sems.at[2 + n])
        for n in range(orbitals)
    ]
    scalars = [
        pltpu.make_async_copy(src, dst, scalar_sems.at[i])
        for i, (src, dst) in enumerate(
            [(shift_hbm, shift_ref), (weight_hbm, weight_ref), (owner_hbm, owner_ref)]
        )
    ]
    for load in scalars + loads:
        load.start()
    pl.semaphore_wait(barrier, peers)

    def cross(q):
        return send(
            chunk_of(pot_ref.at[1 - ring.side], q, per), crossed.at[q],
            cross_sems.at[0, q], cross_sems.at[1, q], ring.across(),
        )

    for q in range(per):
        cross(q).start()

    def center(n):
        return send(
            orb_ref.at[n], orb_rows(1, n, HALO, rows),
            pair_sems.at[0, n], pair_sems.at[1, n], ring.across(),
        )

    def edge_up(k, target):
        if k == 0:
            src, dst = local_ref.at[pl.ds(0, HALO)], local.at[pl.ds(last, HALO)]
        elif k <= orbitals:
            src, dst = orb_ref.at[k - 1, pl.ds(0, HALO)], orb_rows(0, k - 1, last, HALO)
        else:
            n = k - 1 - orbitals
            src, dst = orb_rows(1, n, HALO, HALO), orb_rows(1, n, last, HALO)
        return send(src, dst, edge_sems.at[0, 0, k], edge_sems.at[1, 0, k], target)

    def edge_down(k, target):
        if k == 0:
            src, dst = local_ref.at[pl.ds(rows - HALO, HALO)], local.at[pl.ds(0, HALO)]
        elif k <= orbitals:
            src, dst = orb_ref.at[k - 1, pl.ds(rows - HALO, HALO)], orb_rows(0, k - 1, 0, HALO)
        else:
            n = k - 1 - orbitals
            src, dst = orb_rows(1, n, rows, HALO), orb_rows(1, n, 0, HALO)
        return send(src, dst, edge_sems.at[0, 1, k], edge_sems.at[1, 1, k], target)

    own = range(0, 1 + orbitals)
    theirs = range(1 + orbitals, 1 + 2 * orbitals)

    def start_edges(which):
        @pl.when(has_up)
        def _():
            for k in which:
                edge_up(k, ring.up()).start()

        @pl.when(has_down)
        def _():
            for k in which:
                edge_down(k, ring.down()).start()

    def await_edges(which):
        @pl.when(has_up)
        def _():
            for k in which:
                edge_down(k, ring.across()).wait_recv()

        @pl.when(has_down)
        def _():
            for k in which:
                edge_up(k, ring.across()).wait_recv()

    for load in scalars:
        load.wait()
    for n in range(orbitals):
        pack[0, n] = jnp.full((LANES,), shift_ref[n], jnp.float32)
        pack[0, orbitals + n] = jnp.full((LANES,), weight_ref[n].astype(jnp.float32), jnp.float32)
    start_edges(own)
    share = send(pack.at[0], pack.at[1], pair_sems.at[0, orbitals], pair_sems.at[1, orbitals], ring.across())
    share.start()
    for q in range(per, chunks):
        cross(q).start()
    for n in range(orbitals):
        center(n).start()
    gather.clear()

    def clear(start):
        orbs[:, start : start + HALO] = jnp.zeros((PAIR * orbitals, HALO, cells), jnp.float32)
        local[start : start + HALO] = jnp.zeros((HALO, cells), jnp.float32)
        trial[:, start : start + HALO] = jnp.zeros((half, HALO, cells), jnp.float32)

    @pl.when(jnp.logical_not(has_up))
    def _():
        clear(0)

    @pl.when(jnp.logical_not(has_down))
    def _():
        clear(last)

    sweeps.start()
    loads[0].wait()

    def owner_of(q):
        return owner_ref[(ring.side * half + q // per) // kinds]

    def halo_up(t, target):
        return send(
            trial.at[t, pl.ds(HALO, HALO)], trial.at[t, pl.ds(last, HALO)],
            halo_sems.at[0, 0, t], halo_sems.at[1, 0, t], target,
        )

    def halo_down(t, target):
        return send(
            trial.at[t, pl.ds(rows, HALO)], trial.at[t, pl.ds(0, HALO)],
            halo_sems.at[0, 1, t], halo_sems.at[1, 1, t], target,
        )

    def merge(q):
        cross(q).wait_recv()
        value = jnp.where(owner_of(q) == ring.partner, crossed[q], chunk_of(mine, q, per)[...])
        merged[q] = value
        spread.begin(q, jnp.where(owner_of(q) // PAIR == ring.line, value, 0.0))

    def select(q, came):
        return jnp.where(owner_of(q) // PAIR == ring.line, merged[q], came)

    def settle(q):
        place = owner_of(q) // PAIR
        other = jnp.where(place < ring.line, s_left[q], s_right[q])
        chunk_of(trial, q, per, HALO)[...] = jnp.where(place == ring.line, merged[q], other)

        @pl.when(has_up & (q % per == SPLIT - 1))
        def _():
            halo_up(q // per, ring.up()).start()

        @pl.when(has_down & (q % per == per - 1))
        def _():
            halo_down(q // per, ring.down()).start()

    inner, outer = range(HALO, last), (range(0, HALO), range(last, last + HALO))
    spread.run(0, SPREAD_LAG, merge, select, settle)
    share.wait_recv()
    loads[1].wait()
    sweeps.divide(inner, None)
    spread.run(SPREAD_LAG, FORWARD, merge, select, settle)
    for n in range(orbitals):
        center(n).wait_recv()
        start_edges([theirs[n]])
        spread.run(FORWARD + FORWARD_STEP * n, FORWARD + FORWARD_STEP * (n + 1), merge, select, settle)
    first_trial = FORWARD + FORWARD_STEP * orbitals
    for load in loads[2:]:
        load.wait()
    sweeps.combine(inner, True)
    await_edges(own)
    sweeps.divide(outer[0], has_up)
    sweeps.divide(outer[1], has_down)
    begin = max((ring.lines - 1) * SPREAD_LAG + per, first_trial)
    spread.run(first_trial, begin, merge, select, settle)
    await_edges(theirs)
    sweeps.combine(outer[0], False)
    sweeps.combine(outer[1], False)

    def add(q, came):
        return came + chunk_of(part, q, per)[...]

    def across(q):
        return send(
            ours.at[q], theirs_total.at[q], side_sems.at[0, q], side_sems.at[1, q], ring.across()
        )

    def keep(side, q, value):
        owned = owner_ref[(side * half + q // per) // kinds] == ring.me
        chunk_of(out_ref.at[side], q, per)[...] = jnp.where(owned, value, 0.0)

    def finish(q):
        total = r_left[q] + chunk_of(part, q, per)[...] + r_right[q]
        ours[q] = total
        across(q).start()
        keep(ring.side, q, total)

    def item(t, carry):
        @pl.when(has_up)
        def _():
            halo_down(t, ring.across()).wait_recv()

        @pl.when(has_down)
        def _():
            halo_up(t, ring.across()).wait_recv()

        sweeps.run(t)

        @pl.when(t == 0)
        def _():
            spread.run(begin, spread.steps(), merge, select, settle)

        for c in range(per // SPLIT):
            value = sweeps.collect(c)
            part[t, c * HALO : (c + 1) * HALO] = value
            width = cells // SPLIT
            for j in range(SPLIT):
                gather.begin(t * per + c * SPLIT + j, value[:, j * width : (j + 1) * width])
        gather.run((t - 1) * per + 1, t * per + 1, lambda q: None, add, finish)
        return carry

    lax.fori_loop(0, half, item, 0)
    gather.run((half - 1) * per + 1, gather.steps(), lambda q: None, add, finish)

    def sent(which):
        @pl.when(has_up)
        def _():
            for k in which:
                edge_up(k, ring.across()).wait_send()

        @pl.when(has_down)
        def _():
            for k in which:
                edge_down(k, ring.across()).wait_send()

    sent(own)
    sent(theirs)

    @pl.when(has_up)
    def _():
        for t in range(half):
            halo_up(t, ring.across()).wait_send()

    @pl.when(has_down)
    def _():
        for t in range(half):
            halo_down(t, ring.across()).wait_send()

    share.wait_send()
    for n in range(orbitals):
        center(n).wait_send()
    for q in range(chunks):
        cross(q).wait_send()
    spread.drain()
    gather.drain()
    for q in range(chunks):
        across(q).wait_recv()
        keep(1 - ring.side, q, theirs_total[q])
        across(q).wait_send()


def shards(count, grids, potentials, orbitals, local_pot, shifts, occupation, owner):
    _, blocks, kinds, rows, cells = potentials.shape
    batch = blocks * kinds
    half = batch // PAIR
    orbital_count = orbitals.shape[0]
    planes = rows + 2 * HALO
    wide = PAIR * orbital_count
    stored = potentials.reshape(PAIR, half, rows, cells)
    vmem = pl.BlockSpec(memory_space=pltpu.VMEM)
    hbm = pl.BlockSpec(memory_space=pl.ANY)
    f32 = jnp.float32
    dma = pltpu.SemaphoreType.DMA
    chunks = half * (rows // HALO) * SPLIT
    slots = pltpu.VMEM((chunks, HALO, cells // SPLIT), f32)
    big = pltpu.VMEM((planes, wide, cells), f32)
    packed = pltpu.VMEM((planes * wide, cells), jnp.bfloat16)
    response = pl.pallas_call(
        functools.partial(respond_kernel, count, grids, kinds),
        out_shape=pltpu.VMEM((PAIR, half, rows, cells), f32),
        in_specs=[hbm] * 6,
        out_specs=vmem,
        scratch_shapes=[
            pltpu.SMEM(owner.shape, owner.dtype),
            pltpu.SMEM(shifts.shape, shifts.dtype),
            pltpu.SMEM(occupation.shape, occupation.dtype),
            pltpu.VMEM((half, rows, cells), f32),
            slots, slots, slots, slots,
            pltpu.VMEM((half, planes, cells), f32),
            pltpu.VMEM((PAIR * orbital_count, planes, cells), f32),
            pltpu.VMEM((planes, cells), f32),
            pltpu.VMEM((PAIR, 2 * orbital_count, LANES), f32),
            pltpu.VMEM((half, rows, cells), f32),
            pltpu.VMEM((cells // LANES, rows * wide, LANES), f32),
            slots, slots, slots, slots, slots, slots, slots, slots,
            big, big, big, pltpu.VMEM((rows, wide, cells), f32), big, big,
            packed, packed, packed, packed,
            pltpu.VMEM((planes * wide, WIDTH), f32),
            pltpu.VMEM((2 * WIDTH, WIDTH), jnp.bfloat16),
            dma((3,)), dma((2 + orbital_count,)), dma((2, chunks)), dma((4, chunks)), dma((4, chunks)),
            dma((2, 2, half)), dma((2, 2, 1 + 2 * orbital_count)), dma((2, 1 + orbital_count)),
            dma((2, chunks)),
        ],
        compiler_params=pltpu.CompilerParams(collective_id=0, has_side_effects=True),
        name="respond",
    )(owner, shifts, occupation, stored, orbitals, local_pot)
    return response.reshape(1, blocks, kinds, rows, cells)


def solution(mesh):
    in_specs = (
        P("orb", None, None, "grid", None),
        P("orb", "grid", None),
        P("grid", None),
        P("orb"),
        P("orb"),
        P(),
    )
    out_specs = P("orb", None, None, "grid", None)
    body = functools.partial(shards, mesh.shape["orb"], mesh.shape["grid"])
    return jax.shard_map(body, mesh=mesh, in_specs=in_specs, out_specs=out_specs, check_vma=False)
```
